32 devices in a mesh: row: 8 (over y, x, core), col: 4 (over z).
Axes of the slice: x: 2, y: 2, z: 4, core: 2. Of those that a mesh axis runs over, the one named last changes fastest.
Arguments:
- trailing: float32 [6144, 4096], P('row', 'col'), may hold values from -6 to 6
- column_block: bfloat16 [6144, 1024], P('row', 'col'), may hold values from -6 to 6
- row_block: bfloat16 [1024, 4096], P('row', 'col'), may hold values from -0.1875 to 0.1875
- lower_inv: bfloat16 [1024, 1024], replicated, may hold values from -1 to 1, as said below
- upper_inv: bfloat16 [1024, 1024], replicated, may hold values from -2 to 2, as said below
Outputs:
- lower_panel: bfloat16 [6144, 1024], P('row', 'col')
- upper_panel: bfloat16 [1024, 4096], P('row', 'col')
- updated: float32 [6144, 4096], P('row', 'col')
The draws below stay inside these ranges and needn't reach their ends.
Inputs may be any that keep to these rules, and one draw needn't show every extreme that they name: `lower_inv`: lower triangular with ones on the diagonal. `upper_inv`: upper triangular with diagonal entries between 0.5 and 2.
All inputs are finite; a program needn't handle non-finite values.
Results may differ from the reference program's by a relative error of at most 0.0044.
Values may be sent and summed in bfloat16 or wider, within the bound.
A program may use at most 64 MiB of HBM per device.

```python
import jax
import jax.numpy as jnp

NB = 1024
WROWS = 6144
WCOLS = 4096


def off_diagonal(key):
    first = jax.random.fold_in(jax.random.fold_in(key, 7), 0)
    values = jax.random.normal(first, (NB, NB), jnp.float32)
    return jnp.clip(values * NB ** (-0.5), -0.25, 0.25)


def draw_lower_inv(key, part):
    rowids = jnp.arange(NB)[:, None]
    colids = jnp.arange(NB)[None, :]
    values = off_diagonal(key)
    result = jnp.where(rowids > colids, values, jnp.where(rowids == colids, 1.0, 0.0))
    return result.astype(jnp.bfloat16)


def draw_upper_inv(key, part):
    rowids = jnp.arange(NB)[:, None]
    colids = jnp.arange(NB)[None, :]
    values = off_diagonal(jax.random.fold_in(key, 3))
    diag_key = jax.random.fold_in(key, 11)
    scales = jnp.exp(jax.random.uniform(diag_key, (NB, 1), jnp.float32, jnp.log(0.5), jnp.log(2.0)))
    result = jnp.where(rowids < colids, values, jnp.where(rowids == colids, scales, 0.0))
    return result.astype(jnp.bfloat16)


def block_levels(own_key, dims, cuts, smallest, largest):
    factor_of = 1.0
    for axis_at, shards_of in cuts:
        steps = jax.random.uniform(jax.random.fold_in(jax.random.fold_in(own_key, 6), axis_at), (shards_of,), jnp.float32, smallest / len(cuts), largest / len(cuts))
        factor_of = factor_of * jnp.repeat(jnp.exp(steps), dims[axis_at] // shards_of).reshape((-1,) + (1,) * (len(dims) - 1 - axis_at))
    return factor_of


def centred(rng, dims, spread, bound, pieces=(), held_as=jnp.bfloat16):
    values = spread * jax.random.normal(rng, dims, jnp.float32)
    if pieces:
        values = values * block_levels(rng, dims, pieces, -0.22, 0.18)
    return jnp.clip(values, -bound, bound).astype(held_as)


def setup_inputs(seed: int = 0) -> dict:
    arg_keys = jax.random.split(jax.random.key(seed), 6)
    return {
        "trailing": centred(arg_keys[0], (WROWS, WCOLS), 1.0, 6.0, ((0, 8), (1, 4)), jnp.float32),
        "column_block": centred(arg_keys[1], (WROWS, NB), 1.0, 6.0, ((0, 8), (1, 4))),
        "row_block": centred(arg_keys[2], (NB, WCOLS), NB ** -0.5, 0.1875, ((0, 8), (1, 4))),
        "lower_inv": draw_lower_inv(jax.random.fold_in(arg_keys[5], 71), 0),
        "upper_inv": draw_upper_inv(jax.random.fold_in(arg_keys[5], 71), 0),
    }


def reference(trailing, column_block, row_block, lower_inv, upper_inv):
    lower_panel = jnp.dot(column_block, upper_inv, preferred_element_type=jnp.float32).astype(jnp.bfloat16)
    upper_panel = jnp.dot(lower_inv, row_block, preferred_element_type=jnp.float32).astype(jnp.bfloat16)
    updated = trailing - jnp.dot(lower_panel, upper_panel, preferred_element_type=jnp.float32)
    return lower_panel, upper_panel, updated
```

```python
import functools

import jax
import jax.numpy as jnp
from jax import lax
from jax.experimental import pallas as pl
from jax.experimental.pallas import tpu as pltpu
from jax.sharding import PartitionSpec as P

MESH = pl.DeviceIdType.MESH
BLOCK = 256
PARTS = (3, 3, 2)
ROW_CHUNKS = 2


def chunks_of(rows):
    unit = rows // sum(PARTS)
    starts = [sum(PARTS[:k]) * unit for k in range(len(PARTS))]
    return [(start, part * unit) for start, part in zip(starts, PARTS)]


def reach(size, chunk):
    each = (size - 1) // 2
    extra = 1 if size % 2 == 0 else 0
    return (each + extra, each) if chunk % 2 == 0 else (each, each + extra)


def row_slots(chips):
    slots = {}
    for chunk in range(ROW_CHUNKS):
        for way, limit in enumerate(reach(chips, chunk)):
            for step in range(1, limit + 1):
                slots[way, step, chunk] = len(slots)
    return slots


def kernel(
    n_row, n_col,
    trailing, column_block, row_block, lower_inv, upper_inv,
    lower_tile, gathered, uinv, upper, updated,
    strips, linv, lower,
    local_sem, col_send, col_recv, row_send, row_recv, sib_recv, met,
):
    rows, share = column_block.shape
    depth, cols = row_block.shape
    order = lower_inv.shape[0]
    pieces = chunks_of(rows)
    wide = cols // ROW_CHUNKS
    row, col = lax.axis_index("row"), lax.axis_index("col")
    chips = n_row // 2
    half = chips // 2
    core = lax.rem(row, 2)

    def snake(place):
        return place + (place // half) * (chips + half - 1 - 2 * place)

    place = snake(row // 2)

    def chip_at(offset):
        return snake(lax.rem(place + chips + offset, chips))

    sibling = {"row": row + 1 - 2 * core}
    next_row = chip_at(1) * 2 + core
    prev_row = chip_at(-1) * 2 + core
    row_next = {"row": next_row}
    row_prev = {"row": prev_row}
    next_later = next_row > row
    prev_later = prev_row > row
    after = {"col": col + 1}
    before = {"col": col - 1}
    has_after = col < n_col - 1
    has_before = col > 0

    load_l = pltpu.make_async_copy(lower_inv, linv, local_sem.at[0])
    load_u = pltpu.make_async_copy(upper_inv, uinv, local_sem.at[1])
    load_t = pltpu.make_async_copy(trailing, updated, local_sem.at[2])
    mine_c = pltpu.make_async_copy(column_block, gathered.at[col], local_sem.at[3])
    my_rows = pl.ds(pl.multiple_of(row * depth, depth), depth)
    mine_r = pltpu.make_async_copy(row_block, strips.at[my_rows], local_sem.at[4])

    barrier = pltpu.get_barrier_semaphore()

    def greet(device):
        pl.semaphore_signal(barrier, inc=1, device_id=device, device_id_type=MESH)

    def reply(index, device):
        pl.semaphore_signal(met.at[index], inc=1, device_id=device, device_id_type=MESH)

    def await_reply(index):
        pl.semaphore_wait(met.at[index], 1)

    pl.when(has_after)(lambda: greet(after))
    pl.when(next_later)(lambda: greet(row_next))
    pl.when(prev_later)(lambda: greet(row_prev))
    pl.when(core == 0)(lambda: greet(sibling))
    mine_c.start()
    mine_r.start()
    load_l.start()
    load_u.start()
    behind = (col + n_col - 1) // n_col
    below = (row - next_row + n_row) // n_row + (row - prev_row + n_row) // n_row
    early = core + below + behind
    pl.when(early > 0)(lambda: pl.semaphore_wait(barrier, early))
    pl.when(has_before)(lambda: reply(0, before))
    pl.when(prev_row < row)(lambda: reply(1, row_prev))
    pl.when(next_row < row)(lambda: reply(2, row_next))
    pl.when(core == 1)(lambda: reply(3, sibling))

    slots = row_slots(chips)

    def send(src, dst, recv_sem, device):
        pltpu.make_async_remote_copy(
            src_ref=src, dst_ref=dst, send_sem=row_send, recv_sem=recv_sem,
            device_id=device, device_id_type=MESH,
        ).start()

    def arrived(dst, sem):
        pltpu.make_async_copy(dst, dst, sem).wait()

    def col_slot(owner, chunk):
        return gathered.at[owner, pl.ds(*pieces[chunk])]

    def col_copy(way, step, chunk):
        owner = col + (1 - step if way == 0 else step - 1)
        slot = col_slot(owner, chunk)
        straight = step == 1 and way == 1
        return pltpu.make_async_remote_copy(
            src_ref=column_block.at[pl.ds(*pieces[chunk])] if straight else slot,
            dst_ref=slot,
            send_sem=col_send.at[way],
            recv_sem=col_recv.at[owner - way, chunk],
            device_id=after if way == 0 else before,
            device_id_type=MESH,
        )

    def sends(way, step):
        if way == 0:
            return has_after if step == 1 else has_after & (col >= step - 1)
        return has_before if step == 1 else has_before & (col + step - 1 < n_col)

    def takes(way, step):
        return col >= step if way == 0 else col + step < n_col

    def col_own(way, lane):
        @pl.when(sends(way, 1) & (core == lane))
        def _():
            for chunk in range(len(pieces)):
                col_copy(way, 1, chunk).start()

    def col_event(step, chunk):
        for way in range(2):
            @pl.when(takes(way, step))
            def _():
                owner = col - step if way == 0 else col + step
                arrived(col_slot(owner, chunk), col_recv.at[owner - way, chunk])

            if step < n_col - 1:
                @pl.when(sends(way, step + 1))
                def _():
                    col_copy(way, step + 1, chunk).start()

    def drain():
        for count in range(1, n_col):
            block = gathered.at[pl.ds(0, count)]
            pl.when(col + 1 == count)(lambda: arrived(block, col_send.at[0]))
            pl.when(n_col - col == count)(lambda: arrived(block, col_send.at[1]))
        arrived(strips.at[pl.ds(0, (n_row - 1) * depth)], row_send)

    def strip(offset, lane, chunk):
        owner = chip_at(offset) * 2 + lane
        start = pl.multiple_of(owner * depth, depth)
        return strips.at[pl.ds(start, depth), pl.ds(chunk * wide, wide)]

    def row_send_to(way, step, chunk, src):
        offset = (1 - step) if way == 0 else (step - 1)
        send(
            src, strip(offset, core, chunk),
            row_recv.at[slots[way, step, chunk]],
            row_next if way == 0 else row_prev,
        )

    def share_strip(offset, chunk, src):
        send(src, strip(offset, core, chunk), sib_recv.at[chunk], sibling)

    def row_own(chunk):
        src = row_block.at[:, pl.ds(chunk * wide, wide)]
        for way in range(2):
            if reach(chips, chunk)[way] >= 1:
                row_send_to(way, 1, chunk, src)

    def row_event(step, chunk):
        for way in range(2):
            limit = reach(chips, chunk)[way]
            if step <= limit:
                offset = -step if way == 0 else step
                slot = strip(offset, core, chunk)
                arrived(slot, row_recv.at[slots[way, step, chunk]])
                if step < limit:
                    row_send_to(way, step + 1, chunk, slot)
                share_strip(offset, chunk, slot)

    def row_shared(chunk):
        block = strips.at[pl.ds(0, chips * depth), pl.ds(chunk * wide, wide)]
        arrived(block, sib_recv.at[chunk])

    def make_upper(chunk):
        at = pl.ds(chunk * wide, wide)
        for i in range(order // BLOCK):
            end = (i + 1) * BLOCK
            upper[pl.ds(i * BLOCK, BLOCK), at] = jnp.dot(
                linv[pl.ds(i * BLOCK, BLOCK), pl.ds(0, end)],
                strips[pl.ds(0, end), at],
                preferred_element_type=jnp.float32,
            ).astype(jnp.bfloat16)

    def make_lower(chunk):
        at = pl.ds(*pieces[chunk])
        parts = [gathered[k, at] for k in range(n_col)]
        left = jnp.concatenate(parts, axis=1)
        for j in range(order // BLOCK):
            end = (j + 1) * BLOCK
            lower[at, pl.ds(j * BLOCK, BLOCK)] = jnp.dot(
                left[:, :end],
                uinv[pl.ds(0, end), pl.ds(j * BLOCK, BLOCK)],
                preferred_element_type=jnp.float32,
            ).astype(jnp.bfloat16)
        if share % 128 == 0:
            lower_tile[at] = lower[at, pl.ds(pl.multiple_of(col * share, share), share)]
        else:
            for k in range(n_col):
                @pl.when(col == k)
                def _():
                    lower_tile[at] = lower[at, pl.ds(k * share, share)]

    def subtract(chunk):
        at = pl.ds(*pieces[chunk])
        updated[at] -= jnp.dot(lower[at], upper[...], preferred_element_type=jnp.float32)

    col_own(1, 0)
    mine_c.wait()
    pl.when(has_after)(lambda: await_reply(0))
    col_own(0, 0)
    pl.when(next_later)(lambda: await_reply(1))
    pl.when(prev_later)(lambda: await_reply(2))
    for chunk in range(ROW_CHUNKS):
        row_own(chunk)
    load_l.wait()
    col_own(1, 1)
    col_own(0, 1)
    load_t.start()
    pl.when(core == 0)(lambda: await_reply(3))
    for chunk in range(ROW_CHUNKS):
        share_strip(0, chunk, row_block.at[:, pl.ds(chunk * wide, wide)])
    row_depth = max(max(reach(chips, r)) for r in range(ROW_CHUNKS))
    last = len(pieces) - 1
    for chunk in range(max(len(pieces), ROW_CHUNKS)):
        if chunk < ROW_CHUNKS:
            row_event(1, chunk)
        if chunk <= last:
            col_event(1, chunk)
    for step in range(2, row_depth + 1):
        for chunk in range(ROW_CHUNKS):
            row_event(step, chunk)
    mine_r.wait()
    load_u.wait()
    for chunk in range(ROW_CHUNKS):
        row_shared(chunk)
        make_upper(chunk)
    load_t.wait()
    for step in range(2, n_col - 1):
        for chunk in range(len(pieces)):
            col_event(step, chunk)
    for chunk in range(len(pieces)):
        col_event(n_col - 1, chunk)
        if chunk < last:
            make_lower(chunk)
            subtract(chunk)
    drain()


def finish(
    n_col, lower_done, gathered, uinv, upper, partial, lower_tile, upper_tile, updated,
    low, tile, rest, sem,
):
    rows, cols = partial.shape
    share = lower_tile.shape[1]
    depth = upper_tile.shape[0]
    order = uinv.shape[0]
    col = lax.axis_index("col")
    start = pl.multiple_of(lax.axis_index("row") * depth, depth)
    begin, size = chunks_of(rows)[-1]
    at, done = pl.ds(begin, size), pl.ds(0, begin)
    copies = []

    def copy(src, dst):
        copies.append(pltpu.make_async_copy(src, dst, sem.at[len(copies)]))
        copies[-1].start()

    copy(partial.at[done], updated.at[done])
    copy(lower_done.at[done], lower_tile.at[done])
    copy(upper.at[pl.ds(start, depth)], upper_tile)
    left = jnp.concatenate([gathered[k, at] for k in range(n_col)], axis=1)
    for j in range(order // BLOCK):
        end = (j + 1) * BLOCK
        low[:, pl.ds(j * BLOCK, BLOCK)] = jnp.dot(
            left[:, :end],
            uinv[pl.ds(0, end), pl.ds(j * BLOCK, BLOCK)],
            preferred_element_type=jnp.float32,
        ).astype(jnp.bfloat16)
    if share % 128 == 0:
        tile[...] = low[:, pl.ds(pl.multiple_of(col * share, share), share)]
    else:
        for k in range(n_col):
            @pl.when(col == k)
            def _():
                tile[...] = low[:, pl.ds(k * share, share)]
    copy(tile, lower_tile.at[at])
    for j in range(cols // BLOCK):
        across = pl.ds(j * BLOCK, BLOCK)
        rest[:, across] = partial[at, across] - jnp.dot(
            low[...], upper[:, across], preferred_element_type=jnp.float32
        )
        copy(rest.at[:, across], updated.at[at, across])
    for each in copies:
        each.wait()


def on_device(n_row, n_col, trailing, column_block, row_block, lower_inv, upper_inv):
    rows, share = column_block.shape
    depth, cols = row_block.shape
    order = lower_inv.shape[0]
    chips = n_row // 2
    narrow = jnp.bfloat16
    hbm = pl.BlockSpec(memory_space=pltpu.HBM)
    inside = pl.BlockSpec(memory_space=pltpu.VMEM)
    dma = pltpu.SemaphoreType.DMA
    count = len(PARTS)
    last = chunks_of(rows)[-1][1]
    inputs = (trailing, column_block, row_block, lower_inv, upper_inv)
    tile = jax.ShapeDtypeStruct((rows, share), narrow)
    whole = jax.ShapeDtypeStruct((rows, cols), jnp.float32)
    lower_done, gathered, uinv, upper, partial = pl.pallas_call(
        functools.partial(kernel, n_row, n_col),
        out_shape=(
            tile,
            jax.ShapeDtypeStruct((n_col, rows, share), narrow),
            jax.ShapeDtypeStruct((order, order), narrow),
            jax.ShapeDtypeStruct((order, cols), narrow),
            whole,
        ),
        in_specs=[hbm] * 5,
        out_specs=(inside,) * 5,
        scratch_shapes=[
            pltpu.VMEM((order, cols), narrow),
            pltpu.VMEM((order, order), narrow),
            pltpu.VMEM((rows, order), narrow),
            dma((5,)),
            dma((2,)),
            dma((n_col - 1, count)),
            dma,
            dma((len(row_slots(chips)),)),
            dma((ROW_CHUNKS,)),
            pltpu.SemaphoreType.REGULAR((4,)),
        ],
        compiler_params=pltpu.CompilerParams(
            collective_id=0, has_side_effects=True, vmem_limit_bytes=32 << 20
        ),
    )(*(pltpu.with_memory_space_constraint(x, pltpu.HBM) for x in inputs))
    return pl.pallas_call(
        functools.partial(finish, n_col),
        out_shape=(tile, jax.ShapeDtypeStruct((depth, cols), narrow), whole),
        in_specs=[inside] * 5,
        out_specs=(hbm,) * 3,
        scratch_shapes=[
            pltpu.VMEM((last, order), narrow),
            pltpu.VMEM((last, share), narrow),
            pltpu.VMEM((last, cols), jnp.float32),
            dma((4 + cols // BLOCK,)),
        ],
        compiler_params=pltpu.CompilerParams(vmem_limit_bytes=16 << 20),
    )(lower_done, gathered, uinv, upper, partial)


def solution(mesh):
    specs = P("row", "col")
    return jax.shard_map(
        functools.partial(on_device, mesh.shape["row"], mesh.shape["col"]),
        mesh=mesh,
        in_specs=(specs, specs, specs, P(), P()),
        out_specs=(specs,) * 3,
        check_vma=False,
    )
```

```python
import functools

import jax
import jax.numpy as jnp
from jax import lax
from jax.experimental import pallas as pl
from jax.experimental.pallas import tpu as pltpu
from jax.sharding import PartitionSpec as P

MESH = pl.DeviceIdType.MESH
BLOCK = 256
PARTS = (3, 3, 2)
ROW_CHUNKS = 2
DETOUR = 16


def chunks_of(rows):
    unit = rows // sum(PARTS)
    starts = [sum(PARTS[:k]) * unit for k in range(len(PARTS))]
    return [(start, part * unit) for start, part in zip(starts, PARTS)]


def reach(size, chunk):
    each = (size - 1) // 2
    extra = 1 if size % 2 == 0 else 0
    return (each + extra, each) if chunk % 2 == 0 else (each, each + extra)


def row_slots(chips):
    slots = {}
    for chunk in range(ROW_CHUNKS):
        for way, limit in enumerate(reach(chips, chunk)):
            for step in range(1, limit + 1):
                slots[way, step, chunk] = len(slots)
    return slots


def kernel(
    n_row, n_col,
    trailing, column_block, row_block, lower_inv, upper_inv,
    lower_tile, gathered, uinv, upper, updated,
    strips, linv, lower, spare,
    local_sem, col_send, col_recv, row_send, row_recv, sib_recv, spare_send, spare_recv, met,
):
    rows, share = column_block.shape
    depth, cols = row_block.shape
    order = lower_inv.shape[0]
    pieces = chunks_of(rows)
    wide = cols // ROW_CHUNKS
    row, col = lax.axis_index("row"), lax.axis_index("col")
    chips = n_row // 2
    half = chips // 2
    core = lax.rem(row, 2)

    def snake(place):
        return place + (place // half) * (chips + half - 1 - 2 * place)

    place = snake(row // 2)

    def chip_at(offset):
        return snake(lax.rem(place + chips + offset, chips))

    sibling = {"row": row + 1 - 2 * core}
    next_row = chip_at(1) * 2 + core
    prev_row = chip_at(-1) * 2 + core
    row_next = {"row": next_row}
    row_prev = {"row": prev_row}
    next_later = next_row > row
    prev_later = prev_row > row
    after = {"col": col + 1}
    before = {"col": col - 1}
    has_after = col < n_col - 1
    has_before = col > 0

    load_l = pltpu.make_async_copy(lower_inv, linv, local_sem.at[0])
    load_u = pltpu.make_async_copy(upper_inv, uinv, local_sem.at[1])
    load_t = pltpu.make_async_copy(trailing, updated, local_sem.at[2])
    mine_c = pltpu.make_async_copy(column_block, gathered.at[col], local_sem.at[3])
    my_rows = pl.ds(pl.multiple_of(row * depth, depth), depth)
    mine_r = pltpu.make_async_copy(row_block, strips.at[my_rows], local_sem.at[4])

    barrier = pltpu.get_barrier_semaphore()

    def greet(device):
        pl.semaphore_signal(barrier, inc=1, device_id=device, device_id_type=MESH)

    def reply(index, device):
        pl.semaphore_signal(met.at[index], inc=1, device_id=device, device_id_type=MESH)

    def await_reply(index):
        pl.semaphore_wait(met.at[index], 1)

    pl.when(has_after)(lambda: greet(after))
    pl.when(next_later)(lambda: greet(row_next))
    pl.when(prev_later)(lambda: greet(row_prev))
    pl.when(core == 0)(lambda: greet(sibling))
    mine_c.start()
    mine_r.start()
    load_l.start()
    load_u.start()
    behind = (col + n_col - 1) // n_col
    below = (row - next_row + n_row) // n_row + (row - prev_row + n_row) // n_row
    early = core + below + behind
    pl.when(early > 0)(lambda: pl.semaphore_wait(barrier, early))
    pl.when(has_before)(lambda: reply(0, before))
    pl.when(prev_row < row)(lambda: reply(1, row_prev))
    pl.when(next_row < row)(lambda: reply(2, row_next))
    pl.when(core == 1)(lambda: reply(3, sibling))

    slots = row_slots(chips)

    def send(src, dst, recv_sem, device):
        pltpu.make_async_remote_copy(
            src_ref=src, dst_ref=dst, send_sem=row_send, recv_sem=recv_sem,
            device_id=device, device_id_type=MESH,
        ).start()

    def arrived(dst, sem):
        pltpu.make_async_copy(dst, dst, sem).wait()

    turn = rows // DETOUR

    def span(chunk, short):
        start, size = pieces[chunk]
        return pl.ds(start, size - 2 * turn if short else size)

    def col_slot(owner, chunk, short=False):
        return gathered.at[owner, span(chunk, short)]

    def col_copy(way, step, chunk, short=False):
        owner = col + (1 - step if way == 0 else step - 1)
        slot = col_slot(owner, chunk, short)
        straight = step == 1 and way == 1
        return pltpu.make_async_remote_copy(
            src_ref=column_block.at[span(chunk, short)] if straight else slot,
            dst_ref=slot,
            send_sem=col_send.at[way],
            recv_sem=col_recv.at[owner - way, chunk],
            device_id=after if way == 0 else before,
            device_id_type=MESH,
        )

    def sends(way, step):
        if way == 0:
            return has_after if step == 1 else has_after & (col >= step - 1)
        return has_before if step == 1 else has_before & (col + step - 1 < n_col)

    def takes(way, step):
        return col >= step if way == 0 else col + step < n_col

    def col_own(way):
        for short in range(1 + way):
            @pl.when(sends(way, 1) & turns(1, short) if way else sends(way, 1))
            def _():
                for chunk in range(len(pieces)):
                    col_copy(way, 1, chunk, short and chunk == 0).start()

    def turns(at, short):
        here = (place == 0) & (col == at)
        return here if short else (place != 0) | (col != at)

    def turned(side):
        return pl.ds(pieces[0][1] - (2 - side) * turn, turn)

    def turning(side):
        return (place == (chips - 1 if side else 1)) & (col == 1)

    def turn_own():
        @pl.when(turns(1, True))
        def _():
            for side in range(2):
                pltpu.make_async_remote_copy(
                    src_ref=column_block.at[turned(side)], dst_ref=spare.at[side],
                    send_sem=col_send.at[1], recv_sem=spare_recv.at[side],
                    device_id=row_prev if side else row_next, device_id_type=MESH,
                ).start()

    def turn_event(side):
        @pl.when(turning(side))
        def _():
            arrived(spare.at[side], spare_recv.at[side])
            pltpu.make_async_remote_copy(
                src_ref=spare.at[side], dst_ref=gathered.at[1, turned(side)],
                send_sem=spare_send.at[side], recv_sem=spare_recv.at[side],
                device_id={"row": next_row if side else prev_row, "col": col - 1},
                device_id_type=MESH,
            ).start()

    def turn_last(side):
        @pl.when(turns(0, True))
        def _():
            arrived(gathered.at[1, turned(side)], spare_recv.at[side])

    def col_event(step, chunk):
        for way in range(2):
            cut = way == 1 and step == 1 and chunk == 0
            for short in range(1 + cut):
                @pl.when(takes(way, step) & turns(0, short) if cut else takes(way, step))
                def _():
                    owner = col - step if way == 0 else col + step
                    arrived(col_slot(owner, chunk, short), col_recv.at[owner - way, chunk])

            if step < n_col - 1:
                @pl.when(sends(way, step + 1))
                def _():
                    col_copy(way, step + 1, chunk).start()

    def drain():
        for count in range(1, n_col):
            block = gathered.at[pl.ds(0, count)]
            pl.when(col + 1 == count)(lambda: arrived(block, col_send.at[0]))
            pl.when(n_col - col == count)(lambda: arrived(block, col_send.at[1]))
        arrived(strips.at[pl.ds(0, (n_row - 1) * depth)], row_send)
        for side in range(2):
            pl.when(turning(side))(lambda: arrived(spare.at[side], spare_send.at[side]))

    def strip(offset, lane, chunk):
        owner = chip_at(offset) * 2 + lane
        start = pl.multiple_of(owner * depth, depth)
        return strips.at[pl.ds(start, depth), pl.ds(chunk * wide, wide)]

    def row_send_to(way, step, chunk, src):
        offset = (1 - step) if way == 0 else (step - 1)
        send(
            src, strip(offset, core, chunk),
            row_recv.at[slots[way, step, chunk]],
            row_next if way == 0 else row_prev,
        )

    def share_strip(offset, chunk, src):
        send(src, strip(offset, core, chunk), sib_recv.at[chunk], sibling)

    def row_own(chunk):
        src = row_block.at[:, pl.ds(chunk * wide, wide)]
        for way in range(2):
            if reach(chips, chunk)[way] >= 1:
                row_send_to(way, 1, chunk, src)

    def row_event(step, chunk):
        for way in range(2):
            limit = reach(chips, chunk)[way]
            if step <= limit:
                offset = -step if way == 0 else step
                slot = strip(offset, core, chunk)
                arrived(slot, row_recv.at[slots[way, step, chunk]])
                if step < limit:
                    row_send_to(way, step + 1, chunk, slot)
                share_strip(offset, chunk, slot)

    def row_shared(chunk):
        block = strips.at[pl.ds(0, chips * depth), pl.ds(chunk * wide, wide)]
        arrived(block, sib_recv.at[chunk])

    def make_upper(chunk):
        row_shared(chunk)
        at = pl.ds(chunk * wide, wide)
        for i in range(order // BLOCK):
            end = (i + 1) * BLOCK
            upper[pl.ds(i * BLOCK, BLOCK), at] = jnp.dot(
                linv[pl.ds(i * BLOCK, BLOCK), pl.ds(0, end)],
                strips[pl.ds(0, end), at],
                preferred_element_type=jnp.float32,
            ).astype(jnp.bfloat16)

    def make_lower(chunk):
        at = pl.ds(*pieces[chunk])
        parts = [gathered[k, at] for k in range(n_col)]
        left = jnp.concatenate(parts, axis=1)
        for j in range(order // BLOCK):
            end = (j + 1) * BLOCK
            lower[at, pl.ds(j * BLOCK, BLOCK)] = jnp.dot(
                left[:, :end],
                uinv[pl.ds(0, end), pl.ds(j * BLOCK, BLOCK)],
                preferred_element_type=jnp.float32,
            ).astype(jnp.bfloat16)
        if share % 128 == 0:
            lower_tile[at] = lower[at, pl.ds(pl.multiple_of(col * share, share), share)]
        else:
            for k in range(n_col):
                @pl.when(col == k)
                def _():
                    lower_tile[at] = lower[at, pl.ds(k * share, share)]

    def subtract(chunk):
        at = pl.ds(*pieces[chunk])
        updated[at] -= jnp.dot(lower[at], upper[...], preferred_element_type=jnp.float32)

    col_own(1)
    mine_c.wait()
    pl.when(has_after)(lambda: await_reply(0))
    col_own(0)
    pl.when(next_later)(lambda: await_reply(1))
    pl.when(prev_later)(lambda: await_reply(2))
    turn_own()
    for chunk in range(ROW_CHUNKS):
        row_own(chunk)
    load_t.start()
    pl.when(core == 0)(lambda: await_reply(3))
    for chunk in range(ROW_CHUNKS):
        share_strip(0, chunk, row_block.at[:, pl.ds(chunk * wide, wide)])
    row_depth = max(max(reach(chips, r)) for r in range(ROW_CHUNKS))
    last = len(pieces) - 1
    for chunk in range(max(len(pieces), ROW_CHUNKS)):
        if chunk < ROW_CHUNKS:
            row_event(1, chunk)
        if chunk <= last:
            col_event(1, chunk)
    for side in range(2):
        turn_event(side)
    for step in range(2, row_depth + 1):
        for chunk in range(ROW_CHUNKS):
            row_event(step, chunk)
    mine_r.wait()
    load_l.wait()
    load_u.wait()
    waiting = list(range(ROW_CHUNKS))
    for step in range(2, n_col - 1):
        for chunk in range(len(pieces)):
            col_event(step, chunk)
            if step == n_col - 2 and waiting:
                make_upper(waiting.pop(0))
    for chunk in waiting:
        make_upper(chunk)
    load_t.wait()
    for side in range(2):
        turn_last(side)
    for chunk in range(len(pieces)):
        col_event(n_col - 1, chunk)
        if chunk < last:
            make_lower(chunk)
            subtract(chunk)
    drain()


def finish(
    n_col, lower_done, gathered, uinv, upper, partial, lower_tile, upper_tile, updated,
    low, tile, rest, sem,
):
    rows, cols = partial.shape
    share = lower_tile.shape[1]
    depth = upper_tile.shape[0]
    order = uinv.shape[0]
    col = lax.axis_index("col")
    start = pl.multiple_of(lax.axis_index("row") * depth, depth)
    begin, size = chunks_of(rows)[-1]
    at, done = pl.ds(begin, size), pl.ds(0, begin)
    copies = []

    def copy(src, dst):
        copies.append(pltpu.make_async_copy(src, dst, sem.at[len(copies)]))
        copies[-1].start()

    copy(partial.at[done], updated.at[done])
    copy(lower_done.at[done], lower_tile.at[done])
    copy(upper.at[pl.ds(start, depth)], upper_tile)
    left = jnp.concatenate([gathered[k, at] for k in range(n_col)], axis=1)
    for j in range(order // BLOCK):
        end = (j + 1) * BLOCK
        low[:, pl.ds(j * BLOCK, BLOCK)] = jnp.dot(
            left[:, :end],
            uinv[pl.ds(0, end), pl.ds(j * BLOCK, BLOCK)],
            preferred_element_type=jnp.float32,
        ).astype(jnp.bfloat16)
    if share % 128 == 0:
        tile[...] = low[:, pl.ds(pl.multiple_of(col * share, share), share)]
    else:
        for k in range(n_col):
            @pl.when(col == k)
            def _():
                tile[...] = low[:, pl.ds(k * share, share)]
    copy(tile, lower_tile.at[at])
    for j in range(cols // BLOCK):
        across = pl.ds(j * BLOCK, BLOCK)
        rest[:, across] = partial[at, across] - jnp.dot(
            low[...], upper[:, across], preferred_element_type=jnp.float32
        )
        copy(rest.at[:, across], updated.at[at, across])
    for each in copies:
        each.wait()


def on_device(n_row, n_col, trailing, column_block, row_block, lower_inv, upper_inv):
    rows, share = column_block.shape
    depth, cols = row_block.shape
    order = lower_inv.shape[0]
    chips = n_row // 2
    narrow = jnp.bfloat16
    hbm = pl.BlockSpec(memory_space=pltpu.HBM)
    inside = pl.BlockSpec(memory_space=pltpu.VMEM)
    dma = pltpu.SemaphoreType.DMA
    count = len(PARTS)
    last = chunks_of(rows)[-1][1]
    inputs = (trailing, column_block, row_block, lower_inv, upper_inv)
    tile = jax.ShapeDtypeStruct((rows, share), narrow)
    whole = jax.ShapeDtypeStruct((rows, cols), jnp.float32)
    lower_done, gathered, uinv, upper, partial = pl.pallas_call(
        functools.partial(kernel, n_row, n_col),
        out_shape=(
            tile,
            jax.ShapeDtypeStruct((n_col, rows, share), narrow),
            jax.ShapeDtypeStruct((order, order), narrow),
            jax.ShapeDtypeStruct((order, cols), narrow),
            whole,
        ),
        in_specs=[hbm] * 5,
        out_specs=(inside,) * 5,
        scratch_shapes=[
            pltpu.VMEM((order, cols), narrow),
            pltpu.VMEM((order, order), narrow),
            pltpu.VMEM((rows, order), narrow),
            pltpu.VMEM((2, rows // DETOUR, share), narrow),
            dma((5,)),
            dma((2,)),
            dma((n_col - 1, count)),
            dma,
            dma((len(row_slots(chips)),)),
            dma((ROW_CHUNKS,)),
            dma((2,)),
            dma((2,)),
            pltpu.SemaphoreType.REGULAR((4,)),
        ],
        compiler_params=pltpu.CompilerParams(
            collective_id=0, has_side_effects=True, vmem_limit_bytes=32 << 20
        ),
    )(*(pltpu.with_memory_space_constraint(x, pltpu.HBM) for x in inputs))
    return pl.pallas_call(
        functools.partial(finish, n_col),
        out_shape=(tile, jax.ShapeDtypeStruct((depth, cols), narrow), whole),
        in_specs=[inside] * 5,
        out_specs=(hbm,) * 3,
        scratch_shapes=[
            pltpu.VMEM((last, order), narrow),
            pltpu.VMEM((last, share), narrow),
            pltpu.VMEM((last, cols), jnp.float32),
            dma((4 + cols // BLOCK,)),
        ],
        compiler_params=pltpu.CompilerParams(vmem_limit_bytes=16 << 20),
    )(lower_done, gathered, uinv, upper, partial)


def solution(mesh):
    specs = P("row", "col")
    return jax.shard_map(
        functools.partial(on_device, mesh.shape["row"], mesh.shape["col"]),
        mesh=mesh,
        in_specs=(specs, specs, specs, P(), P()),
        out_specs=(specs,) * 3,
        check_vma=False,
    )
```

```python
import functools

import jax
import jax.numpy as jnp
from jax import lax
from jax.experimental import pallas as pl
from jax.experimental.pallas import tpu as pltpu
from jax.sharding import PartitionSpec as P

MESH = pl.DeviceIdType.MESH
BLOCK = 256
PARTS = (3, 3, 2)
ROW_CHUNKS = 2
DETOUR = 16


def chunks_of(rows):
    unit = rows // sum(PARTS)
    starts = [sum(PARTS[:k]) * unit for k in range(len(PARTS))]
    return [(start, part * unit) for start, part in zip(starts, PARTS)]


def reach(size, chunk):
    each = (size - 1) // 2
    extra = 1 if size % 2 == 0 else 0
    return (each + extra, each) if chunk % 2 == 0 else (each, each + extra)


def row_slots(chips):
    slots = {}
    for chunk in range(ROW_CHUNKS):
        for way, limit in enumerate(reach(chips, chunk)):
            for step in range(1, limit + 1):
                slots[way, step, chunk] = len(slots)
    return slots


def kernel(
    n_row, n_col,
    trailing, column_block, row_block, lower_inv, upper_inv,
    lower_tile, gathered, uinv, upper, updated,
    strips, linv, lower, spare,
    local_sem, col_send, col_recv, row_send, row_recv, sib_recv, spare_send, spare_recv, met,
):
    rows, share = column_block.shape
    depth, cols = row_block.shape
    order = lower_inv.shape[0]
    pieces = chunks_of(rows)
    wide = cols // ROW_CHUNKS
    row, col = lax.axis_index("row"), lax.axis_index("col")
    chips = n_row // 2
    half = chips // 2
    core = lax.rem(row, 2)

    def snake(place):
        return place + (place // half) * (chips + half - 1 - 2 * place)

    place = snake(row // 2)

    def chip_at(offset):
        return snake(lax.rem(place + chips + offset, chips))

    sibling = {"row": row + 1 - 2 * core}
    next_row = chip_at(1) * 2 + core
    prev_row = chip_at(-1) * 2 + core
    row_next = {"row": next_row}
    row_prev = {"row": prev_row}
    next_later = next_row > row
    prev_later = prev_row > row
    after = {"col": col + 1}
    before = {"col": col - 1}
    has_after = col < n_col - 1
    has_before = col > 0

    load_l = pltpu.make_async_copy(lower_inv, linv, local_sem.at[0])
    load_u = pltpu.make_async_copy(upper_inv, uinv, local_sem.at[1])
    load_t = pltpu.make_async_copy(trailing, updated, local_sem.at[2])
    mine_c = pltpu.make_async_copy(column_block, gathered.at[col], local_sem.at[3])
    my_rows = pl.ds(pl.multiple_of(row * depth, depth), depth)
    mine_r = pltpu.make_async_copy(row_block, strips.at[my_rows], local_sem.at[4])

    barrier = pltpu.get_barrier_semaphore()

    def greet(device):
        pl.semaphore_signal(barrier, inc=1, device_id=device, device_id_type=MESH)

    odd = lax.rem(col, 2)
    even = odd == 0

    def reply(index, device):
        pl.semaphore_signal(met.at[index], inc=1, device_id=device, device_id_type=MESH)

    def await_reply(index):
        pl.semaphore_wait(met.at[index], 1)

    pl.when(has_after)(lambda: greet(after))
    pl.when(even & next_later)(lambda: greet(row_next))
    pl.when(even & prev_later)(lambda: greet(row_prev))
    pl.when(even & (core == 0))(lambda: greet(sibling))
    mine_c.start()
    mine_r.start()
    load_l.start()
    load_u.start()
    behind = (col + n_col - 1) // n_col
    below = (row - next_row + n_row) // n_row + (row - prev_row + n_row) // n_row
    early = behind + (core + below) * (1 - odd)
    pl.when(early > 0)(lambda: pl.semaphore_wait(barrier, early))
    pl.when(has_before)(lambda: reply(0, before))

    slots = row_slots(chips)

    def send(src, dst, recv_sem, device):
        pltpu.make_async_remote_copy(
            src_ref=src, dst_ref=dst, send_sem=row_send, recv_sem=recv_sem,
            device_id=device, device_id_type=MESH,
        ).start()

    def arrived(dst, sem):
        pltpu.make_async_copy(dst, dst, sem).wait()

    turn = rows // DETOUR

    def span(chunk, short):
        start, size = pieces[chunk]
        return pl.ds(start, size - 2 * turn if short else size)

    def col_slot(owner, chunk, short=False):
        return gathered.at[owner, span(chunk, short)]

    def col_copy(way, step, chunk, short=False):
        owner = col + (1 - step if way == 0 else step - 1)
        slot = col_slot(owner, chunk, short)
        straight = step == 1 and way == 1
        return pltpu.make_async_remote_copy(
            src_ref=column_block.at[span(chunk, short)] if straight else slot,
            dst_ref=slot,
            send_sem=col_send.at[way],
            recv_sem=col_recv.at[owner - way, chunk],
            device_id=after if way == 0 else before,
            device_id_type=MESH,
        )

    def sends(way, step):
        if way == 0:
            return has_after if step == 1 else has_after & (col >= step - 1)
        return has_before if step == 1 else has_before & (col + step - 1 < n_col)

    def takes(way, step):
        return col >= step if way == 0 else col + step < n_col

    def col_own(way):
        for short in range(1 + way):
            @pl.when(sends(way, 1) & turns(1, short) if way else sends(way, 1))
            def _():
                for chunk in range(len(pieces)):
                    col_copy(way, 1, chunk, short and chunk == 0).start()

    def turns(at, short):
        here = (place == 0) & (col == at)
        return here if short else (place != 0) | (col != at)

    def turned(side):
        return pl.ds(pieces[0][1] - (2 - side) * turn, turn)

    def turning(side):
        return (place == (chips - 1 if side else 1)) & (col == 1)

    def turn_own():
        @pl.when(turns(1, True))
        def _():
            for side in range(2):
                pltpu.make_async_remote_copy(
                    src_ref=column_block.at[turned(side)], dst_ref=spare.at[side],
                    send_sem=col_send.at[1], recv_sem=spare_recv.at[side],
                    device_id=row_prev if side else row_next, device_id_type=MESH,
                ).start()

    def turn_event(side):
        @pl.when(turning(side))
        def _():
            arrived(spare.at[side], spare_recv.at[side])
            pltpu.make_async_remote_copy(
                src_ref=spare.at[side], dst_ref=gathered.at[1, turned(side)],
                send_sem=spare_send.at[side], recv_sem=spare_recv.at[side],
                device_id={"row": next_row if side else prev_row, "col": col - 1},
                device_id_type=MESH,
            ).start()

    def turn_last(side):
        @pl.when(turns(0, True))
        def _():
            arrived(gathered.at[1, turned(side)], spare_recv.at[side])

    def col_event(step, chunk, lane=None):
        mine = (core >= 0) if lane is None else (core == lane)
        for way in range(2):
            cut = way == 1 and step == 1 and chunk == 0
            for short in range(1 + cut):
                @pl.when(mine & (takes(way, step) & turns(0, short) if cut else takes(way, step)))
                def _():
                    owner = col - step if way == 0 else col + step
                    arrived(col_slot(owner, chunk, short), col_recv.at[owner - way, chunk])

            if step < n_col - 1:
                @pl.when(mine & sends(way, step + 1))
                def _():
                    col_copy(way, step + 1, chunk).start()

    def drain():
        for count in range(1, n_col):
            block = gathered.at[pl.ds(0, count)]
            pl.when(col + 1 == count)(lambda: arrived(block, col_send.at[0]))
            pl.when(n_col - col == count)(lambda: arrived(block, col_send.at[1]))
        arrived(strips.at[pl.ds(0, (n_row - 1) * depth)], row_send)
        for side in range(2):
            pl.when(turning(side))(lambda: arrived(spare.at[side], spare_send.at[side]))

    def strip(offset, lane, chunk):
        owner = chip_at(offset) * 2 + lane
        start = pl.multiple_of(owner * depth, depth)
        return strips.at[pl.ds(start, depth), pl.ds(chunk * wide, wide)]

    def row_send_to(way, step, chunk, src):
        offset = (1 - step) if way == 0 else (step - 1)
        send(
            src, strip(offset, core, chunk),
            row_recv.at[slots[way, step, chunk]],
            row_next if way == 0 else row_prev,
        )

    def share_strip(offset, chunk, src):
        send(src, strip(offset, core, chunk), sib_recv.at[chunk], sibling)

    def row_own(chunk):
        src = row_block.at[:, pl.ds(chunk * wide, wide)]
        for way in range(2):
            if reach(chips, chunk)[way] >= 1:
                row_send_to(way, 1, chunk, src)

    def row_event(step, chunk):
        for way in range(2):
            limit = reach(chips, chunk)[way]
            if step <= limit:
                offset = -step if way == 0 else step
                slot = strip(offset, core, chunk)
                arrived(slot, row_recv.at[slots[way, step, chunk]])
                if step < limit:
                    row_send_to(way, step + 1, chunk, slot)
                share_strip(offset, chunk, slot)

    def row_shared(chunk):
        block = strips.at[pl.ds(0, chips * depth), pl.ds(chunk * wide, wide)]
        arrived(block, sib_recv.at[chunk])

    def make_upper(chunk):
        row_shared(chunk)
        at = pl.ds(chunk * wide, wide)
        for i in range(order // BLOCK):
            end = (i + 1) * BLOCK
            upper[pl.ds(i * BLOCK, BLOCK), at] = jnp.dot(
                linv[pl.ds(i * BLOCK, BLOCK), pl.ds(0, end)],
                strips[pl.ds(0, end), at],
                preferred_element_type=jnp.float32,
            ).astype(jnp.bfloat16)

    def make_lower(chunk):
        at = pl.ds(*pieces[chunk])
        parts = [gathered[k, at] for k in range(n_col)]
        left = jnp.concatenate(parts, axis=1)
        for j in range(order // BLOCK):
            end = (j + 1) * BLOCK
            lower[at, pl.ds(j * BLOCK, BLOCK)] = jnp.dot(
                left[:, :end],
                uinv[pl.ds(0, end), pl.ds(j * BLOCK, BLOCK)],
                preferred_element_type=jnp.float32,
            ).astype(jnp.bfloat16)
        if share % 128 == 0:
            lower_tile[at] = lower[at, pl.ds(pl.multiple_of(col * share, share), share)]
        else:
            for k in range(n_col):
                @pl.when(col == k)
                def _():
                    lower_tile[at] = lower[at, pl.ds(k * share, share)]

    def subtract(chunk):
        at = pl.ds(*pieces[chunk])
        updated[at] -= jnp.dot(lower[at], upper[...], preferred_element_type=jnp.float32)

    col_own(1)
    pl.when(even & (prev_row < row))(lambda: reply(1, row_prev))
    pl.when(even & (next_row < row))(lambda: reply(1, row_next))
    pl.when(even & (core == 1))(lambda: reply(1, sibling))
    mine_c.wait()
    pl.when(has_after)(lambda: await_reply(0))
    col_own(0)
    late = (3 - core - below) * (1 - odd)
    pl.when(late > 0)(lambda: pl.semaphore_wait(met.at[1], late))

    @pl.when(even & has_after)
    def _():
        for device in (row_next, row_prev, sibling):
            reply(2, device)

    pl.when(odd == 1)(lambda: await_reply(3))
    turn_own()
    for chunk in range(ROW_CHUNKS):
        row_own(chunk)
    load_t.start()
    for chunk in range(ROW_CHUNKS):
        share_strip(0, chunk, row_block.at[:, pl.ds(chunk * wide, wide)])

    @pl.when(even & has_after)
    def _():
        pl.semaphore_wait(met.at[2], 3)
        reply(3, after)

    row_depth = max(max(reach(chips, r)) for r in range(ROW_CHUNKS))
    last = len(pieces) - 1
    row_left = [(step, r) for step in range(1, row_depth + 1) for r in range(ROW_CHUNKS)]
    col_left = [(step, k) for step in range(2, n_col - 1) for k in range(len(pieces))]
    col_event(1, 0, 0)
    row_event(*row_left.pop(0))
    col_event(1, 1)
    col_event(1, 0, 1)
    for chunk in range(2, len(pieces)):
        col_event(1, chunk)
    while row_left and row_left[0][0] == 1:
        row_event(*row_left.pop(0))
    for side in range(2):
        turn_event(side)
    while row_left:
        row_event(*row_left.pop(0))
        if col_left:
            col_event(*col_left.pop(0))
    mine_r.wait()
    load_l.wait()
    load_u.wait()
    for chunk in range(ROW_CHUNKS):
        make_upper(chunk)
        if col_left:
            col_event(*col_left.pop(0))
    for step, chunk in col_left:
        col_event(step, chunk)
    load_t.wait()
    for side in range(2):
        turn_last(side)
    for chunk in range(len(pieces)):
        if chunk == last:
            drain()
        col_event(n_col - 1, chunk)
        if chunk < last:
            make_lower(chunk)
            subtract(chunk)


def finish(
    n_col, lower_done, gathered, uinv, upper, partial, lower_tile, upper_tile, updated,
    low, tile, rest, sem,
):
    rows, cols = partial.shape
    share = lower_tile.shape[1]
    depth = upper_tile.shape[0]
    order = uinv.shape[0]
    col = lax.axis_index("col")
    start = pl.multiple_of(lax.axis_index("row") * depth, depth)
    begin, size = chunks_of(rows)[-1]
    at, done = pl.ds(begin, size), pl.ds(0, begin)

    def copy(index, src, dst):
        pltpu.make_async_copy(src, dst, sem.at[index]).start()

    copy(0, partial.at[done], updated.at[done])
    copy(1, lower_done.at[done], lower_tile.at[done])
    copy(2, upper.at[pl.ds(start, depth)], upper_tile)
    left = jnp.concatenate([gathered[k, at] for k in range(n_col)], axis=1)
    for j in range(order // BLOCK):
        end = (j + 1) * BLOCK
        low[:, pl.ds(j * BLOCK, BLOCK)] = jnp.dot(
            left[:, :end],
            uinv[pl.ds(0, end), pl.ds(j * BLOCK, BLOCK)],
            preferred_element_type=jnp.float32,
        ).astype(jnp.bfloat16)
    if share % 128 == 0:
        tile[...] = low[:, pl.ds(pl.multiple_of(col * share, share), share)]
    else:
        for k in range(n_col):
            @pl.when(col == k)
            def _():
                tile[...] = low[:, pl.ds(k * share, share)]
    copy(1, tile, lower_tile.at[at])
    for j in range(cols // BLOCK):
        across = pl.ds(j * BLOCK, BLOCK)
        rest[:, across] = partial[at, across] - jnp.dot(
            low[...], upper[:, across], preferred_element_type=jnp.float32
        )
        copy(0, rest.at[:, across], updated.at[at, across])
    for index, whole in enumerate((updated, lower_tile, upper_tile)):
        pltpu.make_async_copy(whole, whole, sem.at[index]).wait()


def on_device(n_row, n_col, trailing, column_block, row_block, lower_inv, upper_inv):
    rows, share = column_block.shape
    depth, cols = row_block.shape
    order = lower_inv.shape[0]
    chips = n_row // 2
    narrow = jnp.bfloat16
    hbm = pl.BlockSpec(memory_space=pltpu.HBM)
    inside = pl.BlockSpec(memory_space=pltpu.VMEM)
    dma = pltpu.SemaphoreType.DMA
    count = len(PARTS)
    last = chunks_of(rows)[-1][1]
    inputs = (trailing, column_block, row_block, lower_inv, upper_inv)
    tile = jax.ShapeDtypeStruct((rows, share), narrow)
    whole = jax.ShapeDtypeStruct((rows, cols), jnp.float32)
    lower_done, gathered, uinv, upper, partial = pl.pallas_call(
        functools.partial(kernel, n_row, n_col),
        out_shape=(
            tile,
            jax.ShapeDtypeStruct((n_col, rows, share), narrow),
            jax.ShapeDtypeStruct((order, order), narrow),
            jax.ShapeDtypeStruct((order, cols), narrow),
            whole,
        ),
        in_specs=[hbm] * 5,
        out_specs=(inside,) * 5,
        scratch_shapes=[
            pltpu.VMEM((order, cols), narrow),
            pltpu.VMEM((order, order), narrow),
            pltpu.VMEM((rows, order), narrow),
            pltpu.VMEM((2, rows // DETOUR, share), narrow),
            dma((5,)),
            dma((2,)),
            dma((n_col - 1, count)),
            dma,
            dma((len(row_slots(chips)),)),
            dma((ROW_CHUNKS,)),
            dma((2,)),
            dma((2,)),
            pltpu.SemaphoreType.REGULAR((4,)),
        ],
        compiler_params=pltpu.CompilerParams(
            collective_id=0, has_side_effects=True, vmem_limit_bytes=32 << 20
        ),
    )(*(pltpu.with_memory_space_constraint(x, pltpu.HBM) for x in inputs))
    return pl.pallas_call(
        functools.partial(finish, n_col),
        out_shape=(tile, jax.ShapeDtypeStruct((depth, cols), narrow), whole),
        in_specs=[inside] * 5,
        out_specs=(hbm,) * 3,
        scratch_shapes=[
            pltpu.VMEM((last, order), narrow),
            pltpu.VMEM((last, share), narrow),
            pltpu.VMEM((last, cols), jnp.float32),
            dma((3,)),
        ],
        compiler_params=pltpu.CompilerParams(vmem_limit_bytes=16 << 20),
    )(lower_done, gathered, uinv, upper, partial)


def solution(mesh):
    specs = P("row", "col")
    return jax.shard_map(
        functools.partial(on_device, mesh.shape["row"], mesh.shape["col"]),
        mesh=mesh,
        in_specs=(specs, specs, specs, P(), P()),
        out_specs=(specs,) * 3,
        check_vma=False,
    )
```

```python
import functools

import jax
import jax.numpy as jnp
from jax import lax
from jax.experimental import pallas as pl
from jax.experimental.pallas import tpu as pltpu
from jax.sharding import PartitionSpec as P

MESH = pl.DeviceIdType.MESH
BLOCK = 256
PARTS = (3, 3, 2)
ROW_CHUNKS = 2
DETOUR = 16


def chunks_of(rows):
    unit = rows // sum(PARTS)
    starts = [sum(PARTS[:k]) * unit for k in range(len(PARTS))]
    return [(start, part * unit) for start, part in zip(starts, PARTS)]


def reach(size, chunk):
    each = (size - 1) // 2
    extra = 1 if size % 2 == 0 else 0
    return (each + extra, each) if chunk % 2 == 0 else (each, each + extra)


def strips_due(chips, step):
    return sum(limit >= step for r in range(ROW_CHUNKS) for limit in reach(chips, r))


def kernel(
    n_row, n_col,
    trailing, column_block, row_block, lower_inv, upper_inv,
    lower_tile, gathered, uinv, upper, updated,
    strips, linv, lower, spare,
    local_sem, col_send, col_recv, row_send, row_recv, sib_recv, spare_send, spare_recv, met,
):
    rows, share = column_block.shape
    depth, cols = row_block.shape
    order = lower_inv.shape[0]
    pieces = chunks_of(rows)
    wide = cols // ROW_CHUNKS
    row, col = lax.axis_index("row"), lax.axis_index("col")
    chips = n_row // 2
    half = chips // 2
    core = lax.rem(row, 2)

    def snake(place):
        return place + (place // half) * (chips + half - 1 - 2 * place)

    place = snake(row // 2)

    def chip_at(offset):
        return snake(lax.rem(place + chips + offset, chips))

    sibling = {"row": row + 1 - 2 * core}
    next_row = chip_at(1) * 2 + core
    prev_row = chip_at(-1) * 2 + core
    row_next = {"row": next_row}
    row_prev = {"row": prev_row}
    next_later = next_row > row
    prev_later = prev_row > row
    after = {"col": col + 1}
    before = {"col": col - 1}
    has_after = col < n_col - 1
    has_before = col > 0

    load_l = pltpu.make_async_copy(lower_inv, linv, local_sem.at[0])
    load_u = pltpu.make_async_copy(upper_inv, uinv, local_sem.at[1])
    load_t = pltpu.make_async_copy(trailing, updated, local_sem.at[2])
    mine_c = pltpu.make_async_copy(column_block, gathered.at[col], local_sem.at[3])
    my_rows = pl.ds(pl.multiple_of(row * depth, depth), depth)
    mine_r = pltpu.make_async_copy(row_block, strips.at[my_rows], local_sem.at[4])

    barrier = pltpu.get_barrier_semaphore()

    def greet(device):
        pl.semaphore_signal(barrier, inc=1, device_id=device, device_id_type=MESH)

    odd = lax.rem(col, 2)
    even = odd == 0
    held = even & (core == 1)
    free = (odd == 1) | (core == 0)

    def reply(index, device):
        pl.semaphore_signal(met.at[index], inc=1, device_id=device, device_id_type=MESH)

    def await_reply(index):
        pl.semaphore_wait(met.at[index], 1)

    pl.when(has_after)(lambda: greet(after))
    pl.when(even & next_later)(lambda: greet(row_next))
    pl.when(even & prev_later)(lambda: greet(row_prev))
    pl.when(even & (core == 0))(lambda: greet(sibling))
    mine_c.start()
    mine_r.start()
    pl.when(free)(lambda: load_l.start())
    load_u.start()
    behind = (col + n_col - 1) // n_col
    below = (row - next_row + n_row) // n_row + (row - prev_row + n_row) // n_row
    early = behind + (core + below) * (1 - odd)
    pl.when(early > 0)(lambda: pl.semaphore_wait(barrier, early))
    pl.when(has_before)(lambda: reply(0, before))


    def send(src, dst, recv_sem, device):
        pltpu.make_async_remote_copy(
            src_ref=src, dst_ref=dst, send_sem=row_send, recv_sem=recv_sem,
            device_id=device, device_id_type=MESH,
        ).start()

    def arrived(dst, sem):
        pltpu.make_async_copy(dst, dst, sem).wait()

    turn = rows // DETOUR

    def span(chunk, short):
        start, size = pieces[chunk]
        return pl.ds(start, size - 2 * turn if short else size)

    def col_slot(owner, chunk, short=False):
        return gathered.at[owner, span(chunk, short)]

    def col_copy(way, step, chunk, short=False):
        owner = col + (1 - step if way == 0 else step - 1)
        slot = col_slot(owner, chunk, short)
        straight = step == 1 and way == 1
        return pltpu.make_async_remote_copy(
            src_ref=column_block.at[span(chunk, short)] if straight else slot,
            dst_ref=slot,
            send_sem=col_send.at[way],
            recv_sem=col_recv.at[owner - way, chunk],
            device_id=after if way == 0 else before,
            device_id_type=MESH,
        )

    def sends(way, step):
        if way == 0:
            return has_after if step == 1 else has_after & (col >= step - 1)
        return has_before if step == 1 else has_before & (col + step - 1 < n_col)

    def takes(way, step):
        return col >= step if way == 0 else col + step < n_col

    def col_own(way):
        for short in range(1 + way):
            @pl.when(sends(way, 1) & turns(1, short) if way else sends(way, 1))
            def _():
                for chunk in range(len(pieces)):
                    col_copy(way, 1, chunk, short and chunk == 0).start()

    def turns(at, short):
        here = (place == 0) & (col == at)
        return here if short else (place != 0) | (col != at)

    def turned(side):
        return pl.ds(pieces[0][1] - (2 - side) * turn, turn)

    def turning(side):
        return (place == (chips - 1 if side else 1)) & (col == 1)

    def turn_own():
        @pl.when(turns(1, True))
        def _():
            for side in range(2):
                pltpu.make_async_remote_copy(
                    src_ref=column_block.at[turned(side)], dst_ref=spare.at[side],
                    send_sem=col_send.at[1], recv_sem=spare_recv.at[side],
                    device_id=row_prev if side else row_next, device_id_type=MESH,
                ).start()

    def turn_event(side):
        @pl.when(turning(side))
        def _():
            arrived(spare.at[side], spare_recv.at[side])
            pltpu.make_async_remote_copy(
                src_ref=spare.at[side], dst_ref=gathered.at[1, turned(side)],
                send_sem=spare_send.at[side], recv_sem=spare_recv.at[side],
                device_id={"row": next_row if side else prev_row, "col": col - 1},
                device_id_type=MESH,
            ).start()

    def turn_last(side):
        @pl.when(turns(0, True))
        def _():
            arrived(gathered.at[1, turned(side)], spare_recv.at[side])

    def lanes(lane):
        return (core >= 0) if lane is None else (core == lane)

    def col_wait(step, chunk, lane=None):
        mine = lanes(lane)
        for way in range(2):
            cut = way == 1 and step == 1 and chunk == 0
            for short in range(1 + cut):
                @pl.when(mine & (takes(way, step) & turns(0, short) if cut else takes(way, step)))
                def _():
                    owner = col - step if way == 0 else col + step
                    arrived(col_slot(owner, chunk, short), col_recv.at[owner - way, chunk])

    def col_pass(step, chunk, lane=None):
        if step < n_col - 1:
            for way in range(2):
                @pl.when(lanes(lane) & sends(way, step + 1))
                def _():
                    col_copy(way, step + 1, chunk).start()

    def col_event(step, chunk, lane=None):
        col_wait(step, chunk, lane)
        col_pass(step, chunk, lane)

    def drain():
        for count in range(1, n_col):
            block = gathered.at[pl.ds(0, count)]
            pl.when(col + 1 == count)(lambda: arrived(block, col_send.at[0]))
            pl.when(n_col - col == count)(lambda: arrived(block, col_send.at[1]))
        arrived(strips.at[pl.ds(0, (n_row - 1) * depth)], row_send)
        for side in range(2):
            pl.when(turning(side))(lambda: arrived(spare.at[side], spare_send.at[side]))

    def strip(offset, lane, chunk):
        owner = chip_at(offset) * 2 + lane
        start = pl.multiple_of(owner * depth, depth)
        return strips.at[pl.ds(start, depth), pl.ds(chunk * wide, wide)]

    def row_send_to(way, step, chunk, src):
        offset = (1 - step) if way == 0 else (step - 1)
        send(
            src, strip(offset, core, chunk),
            row_recv.at[step - 1],
            row_next if way == 0 else row_prev,
        )

    def share_strip(offset, chunk, src):
        send(src, strip(offset, core, chunk), sib_recv, sibling)

    def row_own(chunk):
        src = row_block.at[:, pl.ds(chunk * wide, wide)]
        for way in range(2):
            if reach(chips, chunk)[way] >= 1:
                row_send_to(way, 1, chunk, src)

    def row_event(step):
        due = strips_due(chips, step) * wide // cols
        arrived(strips.at[pl.ds(0, due * depth)], row_recv.at[step - 1])
        for chunk in range(ROW_CHUNKS):
            for way, limit in enumerate(reach(chips, chunk)):
                if step <= limit:
                    offset = -step if way == 0 else step
                    slot = strip(offset, core, chunk)
                    if step < limit:
                        row_send_to(way, step + 1, chunk, slot)
                    share_strip(offset, chunk, slot)

    def make_upper(chunk):
        at = pl.ds(chunk * wide, wide)
        for i in range(order // BLOCK):
            end = (i + 1) * BLOCK
            upper[pl.ds(i * BLOCK, BLOCK), at] = jnp.dot(
                linv[pl.ds(i * BLOCK, BLOCK), pl.ds(0, end)],
                strips[pl.ds(0, end), at],
                preferred_element_type=jnp.float32,
            ).astype(jnp.bfloat16)

    def make_lower(chunk):
        at = pl.ds(*pieces[chunk])
        parts = [gathered[k, at] for k in range(n_col)]
        left = jnp.concatenate(parts, axis=1)
        for j in range(order // BLOCK):
            end = (j + 1) * BLOCK
            lower[at, pl.ds(j * BLOCK, BLOCK)] = jnp.dot(
                left[:, :end],
                uinv[pl.ds(0, end), pl.ds(j * BLOCK, BLOCK)],
                preferred_element_type=jnp.float32,
            ).astype(jnp.bfloat16)
        if share % 128 == 0:
            lower_tile[at] = lower[at, pl.ds(pl.multiple_of(col * share, share), share)]
        else:
            for k in range(n_col):
                @pl.when(col == k)
                def _():
                    lower_tile[at] = lower[at, pl.ds(k * share, share)]

    def subtract(chunk):
        at = pl.ds(*pieces[chunk])
        updated[at] -= jnp.dot(lower[at], upper[...], preferred_element_type=jnp.float32)

    col_own(1)
    pl.when(even & (prev_row < row))(lambda: reply(1, row_prev))
    pl.when(even & (next_row < row))(lambda: reply(1, row_next))
    pl.when(even & (core == 1))(lambda: reply(1, sibling))
    mine_c.wait()
    pl.when(has_after)(lambda: await_reply(0))
    col_own(0)
    late = (3 - core - below) * (1 - odd)
    pl.when(late > 0)(lambda: pl.semaphore_wait(met.at[1], late))

    @pl.when(even & has_after)
    def _():
        for device in (row_next, row_prev, sibling):
            reply(2, device)

    pl.when(odd == 1)(lambda: await_reply(3))
    turn_own()
    for chunk in range(ROW_CHUNKS):
        row_own(chunk)
    load_t.start()
    for chunk in range(ROW_CHUNKS):
        share_strip(0, chunk, row_block.at[:, pl.ds(chunk * wide, wide)])

    @pl.when(even & has_after)
    def _():
        pl.semaphore_wait(met.at[2], 3)
        reply(3, after)

    row_depth = max(max(reach(chips, r)) for r in range(ROW_CHUNKS))
    last = len(pieces) - 1
    col_left = [(step, k) for step in range(2, n_col - 1) for k in range(len(pieces))]
    for chunk in range(2):
        col_event(1, chunk, 0)
    col_wait(1, 1, 1)

    @pl.when(held)
    def _():
        load_l.start()
        load_l.wait()

    col_event(1, 0, 1)
    col_pass(1, 1, 1)
    for chunk in range(2, len(pieces)):
        col_event(1, chunk)
    row_event(1)
    for side in range(2):
        turn_event(side)
    for step in range(2, row_depth + 1):
        if col_left:
            col_event(*col_left.pop(0))
        row_event(step)
    if col_left:
        col_event(*col_left.pop(0))
    arrived(strips.at[pl.ds(0, chips * depth)], sib_recv)
    mine_r.wait()
    pl.when(free)(lambda: load_l.wait())
    load_u.wait()
    for chunk in range(ROW_CHUNKS):
        make_upper(chunk)
        if col_left:
            col_event(*col_left.pop(0))
    for step, chunk in col_left:
        col_event(step, chunk)
    load_t.wait()
    for side in range(2):
        turn_last(side)
    for chunk in range(len(pieces)):
        if chunk == last:
            drain()
        col_event(n_col - 1, chunk)
        if chunk < last:
            make_lower(chunk)
            subtract(chunk)


def finish(
    n_col, lower_done, gathered, uinv, upper, partial, lower_tile, upper_tile, updated,
    low, tile, rest, sem,
):
    rows, cols = partial.shape
    share = lower_tile.shape[1]
    depth = upper_tile.shape[0]
    order = uinv.shape[0]
    col = lax.axis_index("col")
    start = pl.multiple_of(lax.axis_index("row") * depth, depth)
    begin, size = chunks_of(rows)[-1]
    at, done = pl.ds(begin, size), pl.ds(0, begin)

    def copy(index, src, dst):
        pltpu.make_async_copy(src, dst, sem.at[index]).start()

    copy(0, partial.at[done], updated.at[done])
    copy(1, lower_done.at[done], lower_tile.at[done])
    copy(2, upper.at[pl.ds(start, depth)], upper_tile)
    left = jnp.concatenate([gathered[k, at] for k in range(n_col)], axis=1)
    for j in range(order // BLOCK):
        end = (j + 1) * BLOCK
        low[:, pl.ds(j * BLOCK, BLOCK)] = jnp.dot(
            left[:, :end],
            uinv[pl.ds(0, end), pl.ds(j * BLOCK, BLOCK)],
            preferred_element_type=jnp.float32,
        ).astype(jnp.bfloat16)
    if share % 128 == 0:
        tile[...] = low[:, pl.ds(pl.multiple_of(col * share, share), share)]
    else:
        for k in range(n_col):
            @pl.when(col == k)
            def _():
                tile[...] = low[:, pl.ds(k * share, share)]
    copy(1, tile, lower_tile.at[at])
    for j in range(cols // BLOCK):
        across = pl.ds(j * BLOCK, BLOCK)
        rest[:, across] = partial[at, across] - jnp.dot(
            low[...], upper[:, across], preferred_element_type=jnp.float32
        )
        copy(0, rest.at[:, across], updated.at[at, across])
    for index, whole in enumerate((updated, lower_tile, upper_tile)):
        pltpu.make_async_copy(whole, whole, sem.at[index]).wait()


def on_device(n_row, n_col, trailing, column_block, row_block, lower_inv, upper_inv):
    rows, share = column_block.shape
    depth, cols = row_block.shape
    order = lower_inv.shape[0]
    chips = n_row // 2
    narrow = jnp.bfloat16
    hbm = pl.BlockSpec(memory_space=pltpu.HBM)
    inside = pl.BlockSpec(memory_space=pltpu.VMEM)
    dma = pltpu.SemaphoreType.DMA
    count = len(PARTS)
    last = chunks_of(rows)[-1][1]
    inputs = (trailing, column_block, row_block, lower_inv, upper_inv)
    tile = jax.ShapeDtypeStruct((rows, share), narrow)
    whole = jax.ShapeDtypeStruct((rows, cols), jnp.float32)
    lower_done, gathered, uinv, upper, partial = pl.pallas_call(
        functools.partial(kernel, n_row, n_col),
        out_shape=(
            tile,
            jax.ShapeDtypeStruct((n_col, rows, share), narrow),
            jax.ShapeDtypeStruct((order, order), narrow),
            jax.ShapeDtypeStruct((order, cols), narrow),
            whole,
        ),
        in_specs=[hbm] * 5,
        out_specs=(inside,) * 5,
        scratch_shapes=[
            pltpu.VMEM((order, cols), narrow),
            pltpu.VMEM((order, order), narrow),
            pltpu.VMEM((rows, order), narrow),
            pltpu.VMEM((2, rows // DETOUR, share), narrow),
            dma((5,)),
            dma((2,)),
            dma((n_col - 1, count)),
            dma,
            dma((chips // 2,)),
            dma,
            dma((2,)),
            dma((2,)),
            pltpu.SemaphoreType.REGULAR((4,)),
        ],
        compiler_params=pltpu.CompilerParams(
            collective_id=0, has_side_effects=True, vmem_limit_bytes=32 << 20
        ),
    )(*(pltpu.with_memory_space_constraint(x, pltpu.HBM) for x in inputs))
    return pl.pallas_call(
        functools.partial(finish, n_col),
        out_shape=(tile, jax.ShapeDtypeStruct((depth, cols), narrow), whole),
        in_specs=[inside] * 5,
        out_specs=(hbm,) * 3,
        scratch_shapes=[
            pltpu.VMEM((last, order), narrow),
            pltpu.VMEM((last, share), narrow),
            pltpu.VMEM((last, cols), jnp.float32),
            dma((3,)),
        ],
        compiler_params=pltpu.CompilerParams(vmem_limit_bytes=16 << 20),
    )(lower_done, gathered, uinv, upper, partial)


def solution(mesh):
    specs = P("row", "col")
    return jax.shard_map(
        functools.partial(on_device, mesh.shape["row"], mesh.shape["col"]),
        mesh=mesh,
        in_specs=(specs, specs, specs, P(), P()),
        out_specs=(specs,) * 3,
        check_vma=False,
    )
```

```python
import functools

import jax
import jax.numpy as jnp
from jax import lax
from jax.experimental import pallas as pl
from jax.experimental.pallas import tpu as pltpu
from jax.sharding import PartitionSpec as P

MESH = pl.DeviceIdType.MESH
BLOCK = 256
PARTS = (3, 3, 2)
ROW_CHUNKS = 2
DETOUR = 24


def chunks_of(rows):
    unit = rows // sum(PARTS)
    starts = [sum(PARTS[:k]) * unit for k in range(len(PARTS))]
    return [(start, part * unit) for start, part in zip(starts, PARTS)]


def reach(size, chunk):
    each = (size - 1) // 2
    extra = 1 if size % 2 == 0 else 0
    return (each + extra, each) if chunk % 2 == 0 else (each, each + extra)


def strips_due(chips, step):
    return sum(limit >= step for r in range(ROW_CHUNKS) for limit in reach(chips, r))


def turn_stops(chips):
    stops = [(1,), (chips - 1,), (1, 2)]
    return stops if chips > 3 else stops[:2]


def kernel(
    n_row, n_col,
    trailing, column_block, row_block, lower_inv, upper_inv,
    lower_tile, gathered, uinv, upper, updated,
    strips, linv, lower, spare,
    local_sem, col_send, col_recv, row_send, row_recv, sib_recv, spare_send, spare_recv, met,
):
    rows, share = column_block.shape
    depth, cols = row_block.shape
    order = lower_inv.shape[0]
    pieces = chunks_of(rows)
    wide = cols // ROW_CHUNKS
    row, col = lax.axis_index("row"), lax.axis_index("col")
    chips = n_row // 2
    core = lax.rem(row, 2)
    after = {"col": col + 1}
    before = {"col": col - 1}
    has_after = col < n_col - 1
    has_before = col > 0

    barrier = pltpu.get_barrier_semaphore()

    def greet(device):
        pl.semaphore_signal(barrier, inc=1, device_id=device, device_id_type=MESH)

    odd = lax.rem(col, 2)
    even = odd == 0
    held = even & (core == 1)
    free = (odd == 1) | (core == 0)

    def reply(index, device):
        pl.semaphore_signal(met.at[index], inc=1, device_id=device, device_id_type=MESH)

    def await_reply(index):
        pl.semaphore_wait(met.at[index], 1)

    pl.when(has_after)(lambda: greet(after))

    @pl.when(odd == 1)
    def _():
        pl.semaphore_wait(barrier, 1)
        reply(0, before)


    def arrived(dst, sem):
        pltpu.make_async_copy(dst, dst, sem).wait()

    turn = rows // DETOUR
    stops = turn_stops(chips)

    def span(chunk, short):
        start, size = pieces[chunk]
        return pl.ds(start, size - len(stops) * turn if short else size)

    def col_slot(owner, chunk, short=False):
        return gathered.at[owner, span(chunk, short)]

    def col_copy(way, step, chunk, short=False):
        owner = col + (1 - step if way == 0 else step - 1)
        slot = col_slot(owner, chunk, short)
        straight = step == 1 and way == 1
        return pltpu.make_async_remote_copy(
            src_ref=column_block.at[span(chunk, short)] if straight else slot,
            dst_ref=slot,
            send_sem=col_send.at[way],
            recv_sem=col_recv.at[owner - way, chunk],
            device_id=after if way == 0 else before,
            device_id_type=MESH,
        )

    def sends(way, step):
        if way == 0:
            return has_after if step == 1 else has_after & (col >= step - 1)
        return has_before if step == 1 else has_before & (col + step - 1 < n_col)

    def takes(way, step):
        return col >= step if way == 0 else col + step < n_col

    def col_own(way, where, bends=0):
        for short in range(1 + bends):
            @pl.when(sends(way, 1) & where & turns(1, short) if bends else sends(way, 1) & where)
            def _():
                for chunk in range(len(pieces)):
                    col_copy(way, 1, chunk, short and chunk == 0).start()

    def turns(at, short):
        return (row < 2) & (col == at) if short else (row >= 2) | (col != at)

    col_own(1, odd == 1, 1)
    half = chips // 2

    def snake(place):
        return place + (place // half) * (chips + half - 1 - 2 * place)

    place = snake(row // 2)

    def chip_at(offset):
        return snake(lax.rem(place + chips + offset, chips))

    sibling = {"row": row + 1 - 2 * core}
    next_row = chip_at(1) * 2 + core
    prev_row = chip_at(-1) * 2 + core
    row_next = {"row": next_row}
    row_prev = {"row": prev_row}
    next_later = next_row > row
    prev_later = prev_row > row
    load_l = pltpu.make_async_copy(lower_inv, linv, local_sem.at[0])
    load_u = pltpu.make_async_copy(upper_inv, uinv, local_sem.at[1])
    load_t = pltpu.make_async_copy(trailing, updated, local_sem.at[2])
    mine_c = pltpu.make_async_copy(column_block, gathered.at[col], local_sem.at[3])
    my_rows = pl.ds(pl.multiple_of(row * depth, depth), depth)
    mine_r = pltpu.make_async_copy(row_block, strips.at[my_rows], local_sem.at[4])

    pl.when(even & next_later)(lambda: greet(row_next))
    pl.when(even & prev_later)(lambda: greet(row_prev))
    pl.when(even & (core == 0))(lambda: greet(sibling))
    mine_c.start()
    mine_r.start()
    pl.when(free)(lambda: load_l.start())
    load_u.start()
    below = (row - next_row + n_row) // n_row + (row - prev_row + n_row) // n_row
    early = ((col + n_col - 1) // n_col + core + below) * (1 - odd)
    pl.when(early > 0)(lambda: pl.semaphore_wait(barrier, early))
    pl.when(even & has_before)(lambda: reply(0, before))
    col_own(1, even)

    def send(src, dst, recv_sem, device):
        pltpu.make_async_remote_copy(
            src_ref=src, dst_ref=dst, send_sem=row_send, recv_sem=recv_sem,
            device_id=device, device_id_type=MESH,
        ).start()

    def turned(side):
        return pl.ds(pieces[0][1] - (len(stops) - side) * turn, turn)

    def turn_copy(side, src, dst, send_sem, device):
        pltpu.make_async_remote_copy(
            src_ref=src, dst_ref=dst, send_sem=send_sem, recv_sem=spare_recv.at[side],
            device_id=device, device_id_type=MESH,
        ).start()

    def turn_own():
        @pl.when(turns(1, True))
        def _():
            for side in range(len(stops)):
                turn_copy(
                    side, column_block.at[turned(side)], spare.at[side], col_send.at[1],
                    row_prev if side == 1 else row_next,
                )

    def turning(stop):
        return (place == stop) & (col == 1)

    def turn_event(side, hop):
        stop = stops[side][hop]

        @pl.when(turning(stop))
        def _():
            arrived(spare.at[side], spare_recv.at[side])
            if hop + 1 < len(stops[side]):
                turn_copy(side, spare.at[side], spare.at[side], spare_send.at[side], row_next)
            else:
                turn_copy(
                    side, spare.at[side], gathered.at[1, turned(side)], spare_send.at[side],
                    {"row": chip_at(-stop) * 2 + core, "col": col - 1},
                )

    def turn_last(side):
        @pl.when(turns(0, True))
        def _():
            arrived(gathered.at[1, turned(side)], spare_recv.at[side])

    def lanes(lane):
        return (core >= 0) if lane is None else (core == lane)

    def col_wait(step, chunk, lane=None):
        mine = lanes(lane)
        for way in range(2):
            cut = way == 1 and step == 1 and chunk == 0
            for short in range(1 + cut):
                @pl.when(mine & (takes(way, step) & turns(0, short) if cut else takes(way, step)))
                def _():
                    owner = col - step if way == 0 else col + step
                    arrived(col_slot(owner, chunk, short), col_recv.at[owner - way, chunk])

    def col_pass(step, chunk, lane=None):
        if step < n_col - 1:
            for way in range(2):
                @pl.when(lanes(lane) & sends(way, step + 1))
                def _():
                    col_copy(way, step + 1, chunk).start()

    def col_event(step, chunk, lane=None):
        col_wait(step, chunk, lane)
        col_pass(step, chunk, lane)

    def drain():
        for count in range(1, n_col):
            block = gathered.at[pl.ds(0, count)]
            pl.when(col + 1 == count)(lambda: arrived(block, col_send.at[0]))
            pl.when(n_col - col == count)(lambda: arrived(block, col_send.at[1]))
        arrived(strips.at[pl.ds(0, (n_row - 1) * depth)], row_send)
        for side in range(len(stops)):
            for stop in stops[side]:
                pl.when(turning(stop))(lambda: arrived(spare.at[side], spare_send.at[side]))

    def strip(offset, lane, chunk):
        owner = chip_at(offset) * 2 + lane
        start = pl.multiple_of(owner * depth, depth)
        return strips.at[pl.ds(start, depth), pl.ds(chunk * wide, wide)]

    def row_send_to(way, step, chunk, src):
        offset = (1 - step) if way == 0 else (step - 1)
        send(
            src, strip(offset, core, chunk),
            row_recv.at[step - 1],
            row_next if way == 0 else row_prev,
        )

    def share_strip(offset, chunk, src):
        send(src, strip(offset, core, chunk), sib_recv, sibling)

    def row_own(chunk):
        src = row_block.at[:, pl.ds(chunk * wide, wide)]
        for way in range(2):
            if reach(chips, chunk)[way] >= 1:
                row_send_to(way, 1, chunk, src)

    def row_event(step):
        due = strips_due(chips, step) * wide // cols
        arrived(strips.at[pl.ds(0, due * depth)], row_recv.at[step - 1])
        for chunk in range(ROW_CHUNKS):
            for way, limit in enumerate(reach(chips, chunk)):
                if step <= limit:
                    offset = -step if way == 0 else step
                    slot = strip(offset, core, chunk)
                    if step < limit:
                        row_send_to(way, step + 1, chunk, slot)
                    share_strip(offset, chunk, slot)

    def make_upper(chunk):
        at = pl.ds(chunk * wide, wide)
        for i in range(order // BLOCK):
            end = (i + 1) * BLOCK
            upper[pl.ds(i * BLOCK, BLOCK), at] = jnp.dot(
                linv[pl.ds(i * BLOCK, BLOCK), pl.ds(0, end)],
                strips[pl.ds(0, end), at],
                preferred_element_type=jnp.float32,
            ).astype(jnp.bfloat16)

    def make_lower(chunk):
        at = pl.ds(*pieces[chunk])
        parts = [gathered[k, at] for k in range(n_col)]
        left = jnp.concatenate(parts, axis=1)
        for j in range(order // BLOCK):
            end = (j + 1) * BLOCK
            lower[at, pl.ds(j * BLOCK, BLOCK)] = jnp.dot(
                left[:, :end],
                uinv[pl.ds(0, end), pl.ds(j * BLOCK, BLOCK)],
                preferred_element_type=jnp.float32,
            ).astype(jnp.bfloat16)
        if share % 128 == 0:
            lower_tile[at] = lower[at, pl.ds(pl.multiple_of(col * share, share), share)]
        else:
            for k in range(n_col):
                @pl.when(col == k)
                def _():
                    lower_tile[at] = lower[at, pl.ds(k * share, share)]

    def subtract(chunk):
        at = pl.ds(*pieces[chunk])
        updated[at] -= jnp.dot(lower[at], upper[...], preferred_element_type=jnp.float32)

    pl.when(even & (prev_row < row))(lambda: reply(1, row_prev))
    pl.when(even & (next_row < row))(lambda: reply(1, row_next))
    pl.when(even & (core == 1))(lambda: reply(1, sibling))
    mine_c.wait()
    pl.when(has_after)(lambda: await_reply(0))
    col_own(0, has_after)
    late = (3 - core - below) * (1 - odd)
    pl.when(late > 0)(lambda: pl.semaphore_wait(met.at[1], late))

    @pl.when(even & has_after)
    def _():
        for device in (row_next, row_prev, sibling):
            reply(2, device)

    pl.when(odd == 1)(lambda: await_reply(3))
    turn_own()
    for chunk in range(ROW_CHUNKS):
        row_own(chunk)
    load_t.start()
    for chunk in range(ROW_CHUNKS):
        share_strip(0, chunk, row_block.at[:, pl.ds(chunk * wide, wide)])

    @pl.when(even & has_after)
    def _():
        pl.semaphore_wait(met.at[2], 3)
        reply(3, after)

    row_depth = max(max(reach(chips, r)) for r in range(ROW_CHUNKS))
    last = len(pieces) - 1
    col_left = [(step, k) for step in range(2, n_col - 1) for k in range(len(pieces))]
    for chunk in range(2):
        col_event(1, chunk, 0)
    col_wait(1, 1, 1)

    @pl.when(held)
    def _():
        load_l.start()
        load_l.wait()

    col_event(1, 0, 1)
    col_pass(1, 1, 1)
    for chunk in range(2, len(pieces)):
        col_event(1, chunk)
    row_event(1)
    for side in range(len(stops)):
        turn_event(side, 0)
    if len(stops) > 2:
        turn_event(2, 1)
    for step in range(2, row_depth + 1):
        if col_left:
            col_event(*col_left.pop(0))
        row_event(step)
    if col_left:
        col_event(*col_left.pop(0))
    arrived(strips.at[pl.ds(0, chips * depth)], sib_recv)
    mine_r.wait()
    pl.when(free)(lambda: load_l.wait())
    load_u.wait()
    for chunk in range(ROW_CHUNKS):
        make_upper(chunk)
        if col_left:
            col_event(*col_left.pop(0))
    for step, chunk in col_left:
        col_event(step, chunk)
    load_t.wait()
    for side in range(len(stops)):
        turn_last(side)
    for chunk in range(len(pieces)):
        if chunk == last:
            drain()
        col_event(n_col - 1, chunk)
        if chunk < last:
            make_lower(chunk)
            subtract(chunk)


def finish(
    n_col, lower_done, gathered, uinv, upper, partial, lower_tile, upper_tile, updated,
    low, tile, rest, sem,
):
    rows, cols = partial.shape
    share = lower_tile.shape[1]
    depth = upper_tile.shape[0]
    order = uinv.shape[0]
    col = lax.axis_index("col")
    start = pl.multiple_of(lax.axis_index("row") * depth, depth)
    begin, size = chunks_of(rows)[-1]
    at, done = pl.ds(begin, size), pl.ds(0, begin)

    def copy(index, src, dst):
        pltpu.make_async_copy(src, dst, sem.at[index]).start()

    copy(0, partial.at[done], updated.at[done])
    copy(1, lower_done.at[done], lower_tile.at[done])
    copy(2, upper.at[pl.ds(start, depth)], upper_tile)
    left = jnp.concatenate([gathered[k, at] for k in range(n_col)], axis=1)
    for j in range(order // BLOCK):
        end = (j + 1) * BLOCK
        low[:, pl.ds(j * BLOCK, BLOCK)] = jnp.dot(
            left[:, :end],
            uinv[pl.ds(0, end), pl.ds(j * BLOCK, BLOCK)],
            preferred_element_type=jnp.float32,
        ).astype(jnp.bfloat16)
    if share % 128 == 0:
        tile[...] = low[:, pl.ds(pl.multiple_of(col * share, share), share)]
    else:
        for k in range(n_col):
            @pl.when(col == k)
            def _():
                tile[...] = low[:, pl.ds(k * share, share)]
    copy(1, tile, lower_tile.at[at])
    for j in range(cols // BLOCK):
        across = pl.ds(j * BLOCK, BLOCK)
        rest[:, across] = partial[at, across] - jnp.dot(
            low[...], upper[:, across], preferred_element_type=jnp.float32
        )
        copy(0, rest.at[:, across], updated.at[at, across])
    for index, whole in enumerate((updated, lower_tile, upper_tile)):
        pltpu.make_async_copy(whole, whole, sem.at[index]).wait()


def on_device(n_row, n_col, trailing, column_block, row_block, lower_inv, upper_inv):
    rows, share = column_block.shape
    depth, cols = row_block.shape
    order = lower_inv.shape[0]
    chips = n_row // 2
    narrow = jnp.bfloat16
    hbm = pl.BlockSpec(memory_space=pltpu.HBM)
    inside = pl.BlockSpec(memory_space=pltpu.VMEM)
    dma = pltpu.SemaphoreType.DMA
    count = len(PARTS)
    last = chunks_of(rows)[-1][1]
    inputs = (trailing, column_block, row_block, lower_inv, upper_inv)
    tile = jax.ShapeDtypeStruct((rows, share), narrow)
    whole = jax.ShapeDtypeStruct((rows, cols), jnp.float32)
    lower_done, gathered, uinv, upper, partial = pl.pallas_call(
        functools.partial(kernel, n_row, n_col),
        out_shape=(
            tile,
            jax.ShapeDtypeStruct((n_col, rows, share), narrow),
            jax.ShapeDtypeStruct((order, order), narrow),
            jax.ShapeDtypeStruct((order, cols), narrow),
            whole,
        ),
        in_specs=[hbm] * 5,
        out_specs=(inside,) * 5,
        scratch_shapes=[
            pltpu.VMEM((order, cols), narrow),
            pltpu.VMEM((order, order), narrow),
            pltpu.VMEM((rows, order), narrow),
            pltpu.VMEM((len(turn_stops(chips)), rows // DETOUR, share), narrow),
            dma((5,)),
            dma((2,)),
            dma((n_col - 1, count)),
            dma,
            dma((chips // 2,)),
            dma,
            dma((len(turn_stops(chips)),)),
            dma((len(turn_stops(chips)),)),
            pltpu.SemaphoreType.REGULAR((4,)),
        ],
        compiler_params=pltpu.CompilerParams(
            collective_id=0, has_side_effects=True, vmem_limit_bytes=32 << 20
        ),
    )(*(pltpu.with_memory_space_constraint(x, pltpu.HBM) for x in inputs))
    return pl.pallas_call(
        functools.partial(finish, n_col),
        out_shape=(tile, jax.ShapeDtypeStruct((depth, cols), narrow), whole),
        in_specs=[inside] * 5,
        out_specs=(hbm,) * 3,
        scratch_shapes=[
            pltpu.VMEM((last, order), narrow),
            pltpu.VMEM((last, share), narrow),
            pltpu.VMEM((last, cols), jnp.float32),
            dma((3,)),
        ],
        compiler_params=pltpu.CompilerParams(vmem_limit_bytes=16 << 20),
    )(lower_done, gathered, uinv, upper, partial)


def solution(mesh):
    specs = P("row", "col")
    return jax.shard_map(
        functools.partial(on_device, mesh.shape["row"], mesh.shape["col"]),
        mesh=mesh,
        in_specs=(specs, specs, specs, P(), P()),
        out_specs=(specs,) * 3,
        check_vma=False,
    )
```

```python
import functools

import jax
import jax.numpy as jnp
from jax import lax
from jax.experimental import pallas as pl
from jax.experimental.pallas import tpu as pltpu
from jax.sharding import PartitionSpec as P

MESH = pl.DeviceIdType.MESH
BLOCK = 256
PARTS = (3, 3, 2)
ROW_CHUNKS = 2
DETOUR = 24


def chunks_of(rows):
    unit = rows // sum(PARTS)
    starts = [sum(PARTS[:k]) * unit for k in range(len(PARTS))]
    return [(start, part * unit) for start, part in zip(starts, PARTS)]


def reach(size, chunk):
    each = (size - 1) // 2
    extra = 1 if size % 2 == 0 else 0
    return (each + extra, each) if chunk % 2 == 0 else (each, each + extra)


def strips_due(chips, step):
    return sum(limit >= step for r in range(ROW_CHUNKS) for limit in reach(chips, r))


def turn_stops(chips):
    return [(1,), (1, 2), (chips - 1,)] if chips > 3 else [(1,), (chips - 1,)]


def turn_groups(chips):
    groups = {}
    for side, stops in enumerate(turn_stops(chips)):
        for hop, stop in enumerate(stops):
            groups.setdefault((hop, stop), []).append(side)
    return [(hop, stop, sides) for (hop, stop), sides in sorted(groups.items())]


def kernel(
    n_row, n_col,
    trailing, column_block, row_block, lower_inv, upper_inv,
    lower_tile, gathered, uinv, upper, updated,
    strips, linv, lower, spare,
    local_sem, col_send, col_recv, row_send, row_recv, sib_recv, spare_send, spare_recv, met,
):
    rows, share = column_block.shape
    depth, cols = row_block.shape
    order = lower_inv.shape[0]
    pieces = chunks_of(rows)
    wide = cols // ROW_CHUNKS
    row, col = lax.axis_index("row"), lax.axis_index("col")
    chips = n_row // 2
    core = lax.rem(row, 2)
    after = {"col": col + 1}
    before = {"col": col - 1}
    has_after = col < n_col - 1
    has_before = col > 0

    barrier = pltpu.get_barrier_semaphore()

    def greet(device):
        pl.semaphore_signal(barrier, inc=1, device_id=device, device_id_type=MESH)

    odd = lax.rem(col, 2)
    even = odd == 0
    held = even & (core == 1)
    free = (odd == 1) | (core == 0)

    def reply(index, device):
        pl.semaphore_signal(met.at[index], inc=1, device_id=device, device_id_type=MESH)

    def await_reply(index):
        pl.semaphore_wait(met.at[index], 1)

    pl.when(has_after)(lambda: greet(after))

    @pl.when(odd == 1)
    def _():
        pl.semaphore_wait(barrier, 1)
        reply(0, before)


    def arrived(dst, sem):
        pltpu.make_async_copy(dst, dst, sem).wait()

    turn = rows // DETOUR
    stops = turn_stops(chips)

    def span(chunk, short):
        start, size = pieces[chunk]
        return pl.ds(start, size - len(stops) * turn if short else size)

    def col_slot(owner, chunk, short=False):
        return gathered.at[owner, span(chunk, short)]

    def col_copy(way, step, chunk, short=False):
        owner = col + (1 - step if way == 0 else step - 1)
        slot = col_slot(owner, chunk, short)
        straight = step == 1 and way == 1
        return pltpu.make_async_remote_copy(
            src_ref=column_block.at[span(chunk, short)] if straight else slot,
            dst_ref=slot,
            send_sem=col_send.at[way],
            recv_sem=col_recv.at[owner - way, chunk],
            device_id=after if way == 0 else before,
            device_id_type=MESH,
        )

    def sends(way, step):
        if way == 0:
            return has_after if step == 1 else has_after & (col >= step - 1)
        return has_before if step == 1 else has_before & (col + step - 1 < n_col)

    def takes(way, step):
        return col >= step if way == 0 else col + step < n_col

    def col_own(way, where, bends=0):
        for short in reversed(range(1 + bends)):
            @pl.when(sends(way, 1) & where & turns(1, short) if bends else sends(way, 1) & where)
            def _():
                for chunk in range(len(pieces)):
                    col_copy(way, 1, chunk, short and chunk == 0).start()

    def turns(at, short):
        return (row < 2) & (col == at) if short else (row >= 2) | (col != at)

    col_own(1, odd == 1, 1)
    half = chips // 2

    def snake(place):
        return place + (place // half) * (chips + half - 1 - 2 * place)

    place = snake(row // 2)

    def chip_at(offset):
        return snake(lax.rem(place + chips + offset, chips))

    sibling = {"row": row + 1 - 2 * core}
    next_row = chip_at(1) * 2 + core
    prev_row = chip_at(-1) * 2 + core
    row_next = {"row": next_row}
    row_prev = {"row": prev_row}
    next_later = next_row > row
    prev_later = prev_row > row
    load_l = pltpu.make_async_copy(lower_inv, linv, local_sem.at[0])
    load_u = pltpu.make_async_copy(upper_inv, uinv, local_sem.at[1])
    load_t = pltpu.make_async_copy(trailing, updated, local_sem.at[2])
    mine_c = pltpu.make_async_copy(column_block, gathered.at[col], local_sem.at[3])
    my_rows = pl.ds(pl.multiple_of(row * depth, depth), depth)
    mine_r = pltpu.make_async_copy(row_block, strips.at[my_rows], local_sem.at[4])

    pl.when(even & next_later)(lambda: greet(row_next))
    pl.when(even & prev_later)(lambda: greet(row_prev))
    pl.when(even & (core == 0))(lambda: greet(sibling))
    mine_c.start()
    mine_r.start()
    pl.when(free)(lambda: load_l.start())
    load_u.start()
    below = (row - next_row + n_row) // n_row + (row - prev_row + n_row) // n_row
    early = ((col + n_col - 1) // n_col + core + below) * (1 - odd)
    pl.when(early > 0)(lambda: pl.semaphore_wait(barrier, early))
    pl.when(even & has_before)(lambda: reply(0, before))
    col_own(1, even)

    def send(src, dst, recv_sem, device):
        pltpu.make_async_remote_copy(
            src_ref=src, dst_ref=dst, send_sem=row_send, recv_sem=recv_sem,
            device_id=device, device_id_type=MESH,
        ).start()

    def turned(side):
        return pl.ds(pieces[0][1] - (len(stops) - side) * turn, turn)

    def turn_copy(src, dst, send_sem, device):
        pltpu.make_async_remote_copy(
            src_ref=src, dst_ref=dst, send_sem=send_sem, recv_sem=spare_recv,
            device_id=device, device_id_type=MESH,
        ).start()

    def turn_own():
        @pl.when(turns(1, True))
        def _():
            for side in range(len(stops)):
                turn_copy(
                    column_block.at[turned(side)], spare.at[side], col_send.at[1],
                    row_next if stops[side][0] == 1 else row_prev,
                )

    def turning(stop):
        return (place == stop) & (col == 1)

    def turn_block(sides):
        return spare.at[pl.ds(sides[0], len(sides))]

    def turn_event(hop, stop, sides):
        @pl.when(turning(stop))
        def _():
            arrived(turn_block(sides), spare_recv)
            for side in sides:
                if hop + 1 < len(stops[side]):
                    turn_copy(spare.at[side], spare.at[side], spare_send, row_next)
                else:
                    turn_copy(
                        spare.at[side], gathered.at[1, turned(side)], spare_send,
                        {"row": chip_at(-stop) * 2 + core, "col": col - 1},
                    )

    def turn_last():
        @pl.when(turns(0, True))
        def _():
            size = len(stops) * turn
            arrived(gathered.at[1, pl.ds(pieces[0][1] - size, size)], spare_recv)

    def lanes(lane):
        return (core >= 0) if lane is None else (core == lane)

    def col_wait(step, chunk, lane=None):
        mine = lanes(lane)
        for way in range(2):
            cut = way == 1 and step == 1 and chunk == 0
            for short in range(1 + cut):
                @pl.when(mine & (takes(way, step) & turns(0, short) if cut else takes(way, step)))
                def _():
                    owner = col - step if way == 0 else col + step
                    arrived(col_slot(owner, chunk, short), col_recv.at[owner - way, chunk])

    def col_pass(step, chunk, lane=None):
        if step < n_col - 1:
            for way in range(2):
                @pl.when(lanes(lane) & sends(way, step + 1))
                def _():
                    col_copy(way, step + 1, chunk).start()

    def col_event(step, chunk, lane=None):
        col_wait(step, chunk, lane)
        col_pass(step, chunk, lane)

    def drain():
        for count in range(1, n_col):
            block = gathered.at[pl.ds(0, count)]
            pl.when(col + 1 == count)(lambda: arrived(block, col_send.at[0]))
            pl.when(n_col - col == count)(lambda: arrived(block, col_send.at[1]))
        arrived(strips.at[pl.ds(0, (n_row - 1) * depth)], row_send)
        for hop, stop, sides in turn_groups(chips):
            pl.when(turning(stop))(lambda: arrived(turn_block(sides), spare_send))

    def strip(offset, lane, chunk):
        owner = chip_at(offset) * 2 + lane
        start = pl.multiple_of(owner * depth, depth)
        return strips.at[pl.ds(start, depth), pl.ds(chunk * wide, wide)]

    def row_send_to(way, step, chunk, src):
        offset = (1 - step) if way == 0 else (step - 1)
        send(
            src, strip(offset, core, chunk),
            row_recv.at[step - 1],
            row_next if way == 0 else row_prev,
        )

    def share_strip(offset, chunk, src):
        send(src, strip(offset, core, chunk), sib_recv, sibling)

    def row_own(chunk):
        src = row_block.at[:, pl.ds(chunk * wide, wide)]
        for way in range(2):
            if reach(chips, chunk)[way] >= 1:
                row_send_to(way, 1, chunk, src)

    def row_event(step):
        due = strips_due(chips, step) * wide // cols
        arrived(strips.at[pl.ds(0, due * depth)], row_recv.at[step - 1])
        for chunk in range(ROW_CHUNKS):
            for way, limit in enumerate(reach(chips, chunk)):
                if step <= limit:
                    offset = -step if way == 0 else step
                    slot = strip(offset, core, chunk)
                    if step < limit:
                        row_send_to(way, step + 1, chunk, slot)
                    share_strip(offset, chunk, slot)

    def make_upper(chunk):
        at = pl.ds(chunk * wide, wide)
        for i in range(order // BLOCK):
            end = (i + 1) * BLOCK
            upper[pl.ds(i * BLOCK, BLOCK), at] = jnp.dot(
                linv[pl.ds(i * BLOCK, BLOCK), pl.ds(0, end)],
                strips[pl.ds(0, end), at],
                preferred_element_type=jnp.float32,
            ).astype(jnp.bfloat16)

    def make_lower(chunk):
        at = pl.ds(*pieces[chunk])
        parts = [gathered[k, at] for k in range(n_col)]
        left = jnp.concatenate(parts, axis=1)
        for j in range(order // BLOCK):
            end = (j + 1) * BLOCK
            lower[at, pl.ds(j * BLOCK, BLOCK)] = jnp.dot(
                left[:, :end],
                uinv[pl.ds(0, end), pl.ds(j * BLOCK, BLOCK)],
                preferred_element_type=jnp.float32,
            ).astype(jnp.bfloat16)
        if share % 128 == 0:
            lower_tile[at] = lower[at, pl.ds(pl.multiple_of(col * share, share), share)]
        else:
            for k in range(n_col):
                @pl.when(col == k)
                def _():
                    lower_tile[at] = lower[at, pl.ds(k * share, share)]

    def subtract(chunk):
        at = pl.ds(*pieces[chunk])
        updated[at] -= jnp.dot(lower[at], upper[...], preferred_element_type=jnp.float32)

    pl.when(even & (prev_row < row))(lambda: reply(1, row_prev))
    pl.when(even & (next_row < row))(lambda: reply(1, row_next))
    pl.when(even & (core == 1))(lambda: reply(1, sibling))
    mine_c.wait()
    pl.when(has_after)(lambda: await_reply(0))
    col_own(0, has_after)
    late = (3 - core - below) * (1 - odd)
    pl.when(late > 0)(lambda: pl.semaphore_wait(met.at[1], late))

    @pl.when(even & has_after)
    def _():
        for device in (row_next, row_prev, sibling):
            reply(2, device)

    pl.when(odd == 1)(lambda: await_reply(1))
    turn_own()
    for chunk in range(ROW_CHUNKS):
        row_own(chunk)
    load_t.start()
    for chunk in range(ROW_CHUNKS):
        share_strip(0, chunk, row_block.at[:, pl.ds(chunk * wide, wide)])

    @pl.when(even & has_after)
    def _():
        pl.semaphore_wait(met.at[2], 3)
        reply(1, after)

    row_depth = max(max(reach(chips, r)) for r in range(ROW_CHUNKS))
    last = len(pieces) - 1
    col_left = [(step, k) for step in range(2, n_col - 1) for k in range(len(pieces))]
    for chunk in range(2):
        col_event(1, chunk, 0)
    col_wait(1, 1, 1)

    @pl.when(held)
    def _():
        load_l.start()
        load_l.wait()

    col_event(1, 0, 1)
    col_pass(1, 1, 1)
    for chunk in range(2, len(pieces)):
        col_event(1, chunk)
    row_event(1)
    for group in turn_groups(chips):
        turn_event(*group)
    for step in range(2, row_depth + 1):
        if col_left:
            col_event(*col_left.pop(0))
        row_event(step)
    if col_left:
        col_event(*col_left.pop(0))
    arrived(strips.at[pl.ds(0, chips * depth)], sib_recv)
    mine_r.wait()
    pl.when(free)(lambda: load_l.wait())
    load_u.wait()
    for chunk in range(ROW_CHUNKS):
        make_upper(chunk)
        if col_left:
            col_event(*col_left.pop(0))
    for step, chunk in col_left:
        col_event(step, chunk)
    load_t.wait()
    turn_last()
    for chunk in range(len(pieces)):
        if chunk == last:
            drain()
        col_event(n_col - 1, chunk)
        if chunk < last:
            make_lower(chunk)
            subtract(chunk)


def finish(
    n_col, lower_done, gathered, uinv, upper, partial, lower_tile, upper_tile, updated,
    low, tile, rest, sem,
):
    rows, cols = partial.shape
    share = lower_tile.shape[1]
    depth = upper_tile.shape[0]
    order = uinv.shape[0]
    col = lax.axis_index("col")
    start = pl.multiple_of(lax.axis_index("row") * depth, depth)
    begin, size = chunks_of(rows)[-1]
    at, done = pl.ds(begin, size), pl.ds(0, begin)

    def copy(index, src, dst):
        pltpu.make_async_copy(src, dst, sem.at[index]).start()

    copy(0, partial.at[done], updated.at[done])
    copy(1, lower_done.at[done], lower_tile.at[done])
    copy(2, upper.at[pl.ds(start, depth)], upper_tile)
    left = jnp.concatenate([gathered[k, at] for k in range(n_col)], axis=1)
    for j in range(order // BLOCK):
        end = (j + 1) * BLOCK
        low[:, pl.ds(j * BLOCK, BLOCK)] = jnp.dot(
            left[:, :end],
            uinv[pl.ds(0, end), pl.ds(j * BLOCK, BLOCK)],
            preferred_element_type=jnp.float32,
        ).astype(jnp.bfloat16)
    if share % 128 == 0:
        tile[...] = low[:, pl.ds(pl.multiple_of(col * share, share), share)]
    else:
        for k in range(n_col):
            @pl.when(col == k)
            def _():
                tile[...] = low[:, pl.ds(k * share, share)]
    copy(1, tile, lower_tile.at[at])
    for j in range(cols // BLOCK):
        across = pl.ds(j * BLOCK, BLOCK)
        rest[:, across] = partial[at, across] - jnp.dot(
            low[...], upper[:, across], preferred_element_type=jnp.float32
        )
        copy(0, rest.at[:, across], updated.at[at, across])
    for index, whole in enumerate((updated, lower_tile, upper_tile)):
        pltpu.make_async_copy(whole, whole, sem.at[index]).wait()


def on_device(n_row, n_col, trailing, column_block, row_block, lower_inv, upper_inv):
    rows, share = column_block.shape
    depth, cols = row_block.shape
    order = lower_inv.shape[0]
    chips = n_row // 2
    narrow = jnp.bfloat16
    hbm = pl.BlockSpec(memory_space=pltpu.HBM)
    inside = pl.BlockSpec(memory_space=pltpu.VMEM)
    dma = pltpu.SemaphoreType.DMA
    count = len(PARTS)
    last = chunks_of(rows)[-1][1]
    inputs = (trailing, column_block, row_block, lower_inv, upper_inv)
    tile = jax.ShapeDtypeStruct((rows, share), narrow)
    whole = jax.ShapeDtypeStruct((rows, cols), jnp.float32)
    lower_done, gathered, uinv, upper, partial = pl.pallas_call(
        functools.partial(kernel, n_row, n_col),
        out_shape=(
            tile,
            jax.ShapeDtypeStruct((n_col, rows, share), narrow),
            jax.ShapeDtypeStruct((order, order), narrow),
            jax.ShapeDtypeStruct((order, cols), narrow),
            whole,
        ),
        in_specs=[hbm] * 5,
        out_specs=(inside,) * 5,
        scratch_shapes=[
            pltpu.VMEM((order, cols), narrow),
            pltpu.VMEM((order, order), narrow),
            pltpu.VMEM((rows, order), narrow),
            pltpu.VMEM((len(turn_stops(chips)), rows // DETOUR, share), narrow),
            dma((5,)),
            dma((2,)),
            dma((n_col - 1, count)),
            dma,
            dma((chips // 2,)),
            dma,
            dma,
            dma,
            pltpu.SemaphoreType.REGULAR((3,)),
        ],
        compiler_params=pltpu.CompilerParams(
            collective_id=0, has_side_effects=True, vmem_limit_bytes=32 << 20
        ),
    )(*(pltpu.with_memory_space_constraint(x, pltpu.HBM) for x in inputs))
    return pl.pallas_call(
        functools.partial(finish, n_col),
        out_shape=(tile, jax.ShapeDtypeStruct((depth, cols), narrow), whole),
        in_specs=[inside] * 5,
        out_specs=(hbm,) * 3,
        scratch_shapes=[
            pltpu.VMEM((last, order), narrow),
            pltpu.VMEM((last, share), narrow),
            pltpu.VMEM((last, cols), jnp.float32),
            dma((3,)),
        ],
        compiler_params=pltpu.CompilerParams(vmem_limit_bytes=16 << 20),
    )(lower_done, gathered, uinv, upper, partial)


def solution(mesh):
    specs = P("row", "col")
    return jax.shard_map(
        functools.partial(on_device, mesh.shape["row"], mesh.shape["col"]),
        mesh=mesh,
        in_specs=(specs, specs, specs, P(), P()),
        out_specs=(specs,) * 3,
        check_vma=False,
    )
```

```python
import functools

import jax
import jax.numpy as jnp
from jax import lax
from jax.experimental import pallas as pl
from jax.experimental.pallas import tpu as pltpu
from jax.sharding import PartitionSpec as P

MESH = pl.DeviceIdType.MESH
BLOCK = 256
PARTS = (5, 4, 3)
ROW_CHUNKS = 2
DETOUR = 24


def chunks_of(rows):
    unit = rows // sum(PARTS)
    starts = [sum(PARTS[:k]) * unit for k in range(len(PARTS))]
    return [(start, part * unit) for start, part in zip(starts, PARTS)]


def reach(size, chunk):
    each = (size - 1) // 2
    extra = 1 if size % 2 == 0 else 0
    return (each + extra, each) if chunk % 2 == 0 else (each, each + extra)


def strips_due(chips, step):
    return sum(limit >= step for r in range(ROW_CHUNKS) for limit in reach(chips, r))


def turn_stops(chips):
    return [(1,), (1, 2), (chips - 1,)] if chips > 3 else [(1,), (chips - 1,)]


def turn_groups(chips):
    groups = {}
    for side, stops in enumerate(turn_stops(chips)):
        for hop, stop in enumerate(stops):
            groups.setdefault((hop, stop), []).append(side)
    return [(hop, stop, sides) for (hop, stop), sides in sorted(groups.items())]


def kernel(
    n_row, n_col,
    trailing, column_block, row_block, lower_inv, upper_inv,
    lower_tile, gathered, uinv, upper, updated,
    strips, linv, lower, spare,
    local_sem, col_send, col_recv, row_send, row_recv, sib_recv, spare_send, spare_recv, met,
):
    rows, share = column_block.shape
    depth, cols = row_block.shape
    order = lower_inv.shape[0]
    pieces = chunks_of(rows)
    wide = cols // ROW_CHUNKS
    row, col = lax.axis_index("row"), lax.axis_index("col")
    chips = n_row // 2
    core = lax.rem(row, 2)
    after = {"col": col + 1}
    before = {"col": col - 1}
    has_after = col < n_col - 1
    has_before = col > 0

    barrier = pltpu.get_barrier_semaphore()

    def greet(device):
        pl.semaphore_signal(barrier, inc=1, device_id=device, device_id_type=MESH)

    odd = lax.rem(col, 2)
    even = odd == 0
    held = even & (core == 1)
    free = (odd == 1) | (core == 0)

    def reply(index, device):
        pl.semaphore_signal(met.at[index], inc=1, device_id=device, device_id_type=MESH)

    def await_reply(index):
        pl.semaphore_wait(met.at[index], 1)

    pl.when(has_after)(lambda: greet(after))

    @pl.when(odd == 1)
    def _():
        pl.semaphore_wait(barrier, 1)
        reply(0, before)


    def arrived(dst, sem):
        pltpu.make_async_copy(dst, dst, sem).wait()

    turn = rows // DETOUR
    stops = turn_stops(chips)

    def span(chunk, short):
        start, size = pieces[chunk]
        return pl.ds(start, size - len(stops) * turn if short else size)

    def col_slot(owner, chunk, short=False):
        return gathered.at[owner, span(chunk, short)]

    def col_copy(way, step, chunk, short=False):
        owner = col + (1 - step if way == 0 else step - 1)
        slot = col_slot(owner, chunk, short)
        straight = step == 1 and way == 1
        return pltpu.make_async_remote_copy(
            src_ref=column_block.at[span(chunk, short)] if straight else slot,
            dst_ref=slot,
            send_sem=col_send.at[way],
            recv_sem=col_recv.at[owner - way, chunk],
            device_id=after if way == 0 else before,
            device_id_type=MESH,
        )

    def sends(way, step):
        if way == 0:
            return has_after if step == 1 else has_after & (col >= step - 1)
        return has_before if step == 1 else has_before & (col + step - 1 < n_col)

    def takes(way, step):
        return col >= step if way == 0 else col + step < n_col

    def col_own(way, where, bends=0):
        for short in reversed(range(1 + bends)):
            @pl.when(sends(way, 1) & where & turns(1, short) if bends else sends(way, 1) & where)
            def _():
                for chunk in range(len(pieces)):
                    col_copy(way, 1, chunk, short and chunk == 0).start()

    def turns(at, short):
        return (row < 2) & (col == at) if short else (row >= 2) | (col != at)

    col_own(1, odd == 1, 1)
    half = chips // 2

    def snake(place):
        return place + (place // half) * (chips + half - 1 - 2 * place)

    place = snake(row // 2)

    def chip_at(offset):
        return snake(lax.rem(place + chips + offset, chips))

    sibling = {"row": row + 1 - 2 * core}
    next_row = chip_at(1) * 2 + core
    prev_row = chip_at(-1) * 2 + core
    row_next = {"row": next_row}
    row_prev = {"row": prev_row}
    next_later = next_row > row
    prev_later = prev_row > row
    load_l = pltpu.make_async_copy(lower_inv, linv, local_sem.at[0])
    load_u = pltpu.make_async_copy(upper_inv, uinv, local_sem.at[1])
    load_t = pltpu.make_async_copy(trailing, updated, local_sem.at[2])
    mine_c = pltpu.make_async_copy(column_block, gathered.at[col], local_sem.at[3])
    my_rows = pl.ds(pl.multiple_of(row * depth, depth), depth)
    mine_r = pltpu.make_async_copy(row_block, strips.at[my_rows], local_sem.at[4])

    pl.when(even & next_later)(lambda: greet(row_next))
    pl.when(even & prev_later)(lambda: greet(row_prev))
    pl.when(even & (core == 0))(lambda: greet(sibling))
    mine_c.start()
    mine_r.start()
    pl.when(free)(lambda: load_l.start())
    load_u.start()
    below = (row - next_row + n_row) // n_row + (row - prev_row + n_row) // n_row
    early = ((col + n_col - 1) // n_col + core + below) * (1 - odd)
    pl.when(early > 0)(lambda: pl.semaphore_wait(barrier, early))
    pl.when(even & has_before)(lambda: reply(0, before))
    col_own(1, even)

    def send(src, dst, recv_sem, device):
        pltpu.make_async_remote_copy(
            src_ref=src, dst_ref=dst, send_sem=row_send, recv_sem=recv_sem,
            device_id=device, device_id_type=MESH,
        ).start()

    def turned(side):
        return pl.ds(pieces[0][1] - (len(stops) - side) * turn, turn)

    def turn_copy(src, dst, send_sem, device):
        pltpu.make_async_remote_copy(
            src_ref=src, dst_ref=dst, send_sem=send_sem, recv_sem=spare_recv,
            device_id=device, device_id_type=MESH,
        ).start()

    def turn_own():
        @pl.when(turns(1, True))
        def _():
            for side in range(len(stops)):
                turn_copy(
                    column_block.at[turned(side)], spare.at[side], col_send.at[1],
                    row_next if stops[side][0] == 1 else row_prev,
                )

    def turning(stop):
        return (place == stop) & (col == 1)

    def turn_block(sides):
        return spare.at[pl.ds(sides[0], len(sides))]

    def turn_event(hop, stop, sides):
        @pl.when(turning(stop))
        def _():
            arrived(turn_block(sides), spare_recv)
            for side in sides:
                if hop + 1 < len(stops[side]):
                    turn_copy(spare.at[side], spare.at[side], spare_send, row_next)
                else:
                    turn_copy(
                        spare.at[side], gathered.at[1, turned(side)], spare_send,
                        {"row": chip_at(-stop) * 2 + core, "col": col - 1},
                    )

    def turn_last():
        @pl.when(turns(0, True))
        def _():
            size = len(stops) * turn
            arrived(gathered.at[1, pl.ds(pieces[0][1] - size, size)], spare_recv)

    def lanes(lane):
        return (core >= 0) if lane is None else (core == lane)

    def col_wait(step, chunk, lane=None):
        mine = lanes(lane)
        for way in range(2):
            cut = way == 1 and step == 1 and chunk == 0
            for short in range(1 + cut):
                @pl.when(mine & (takes(way, step) & turns(0, short) if cut else takes(way, step)))
                def _():
                    owner = col - step if way == 0 else col + step
                    arrived(col_slot(owner, chunk, short), col_recv.at[owner - way, chunk])

    def col_pass(step, chunk, lane=None):
        if step < n_col - 1:
            for way in range(2):
                @pl.when(lanes(lane) & sends(way, step + 1))
                def _():
                    col_copy(way, step + 1, chunk).start()

    def col_event(step, chunk, lane=None):
        col_wait(step, chunk, lane)
        col_pass(step, chunk, lane)

    def drain():
        for count in range(1, n_col):
            block = gathered.at[pl.ds(0, count)]
            pl.when(col + 1 == count)(lambda: arrived(block, col_send.at[0]))
            pl.when(n_col - col == count)(lambda: arrived(block, col_send.at[1]))
        arrived(strips.at[pl.ds(0, (n_row - 1) * depth)], row_send)
        for hop, stop, sides in turn_groups(chips):
            pl.when(turning(stop))(lambda: arrived(turn_block(sides), spare_send))

    def strip(offset, lane, chunk):
        owner = chip_at(offset) * 2 + lane
        start = pl.multiple_of(owner * depth, depth)
        return strips.at[pl.ds(start, depth), pl.ds(chunk * wide, wide)]

    def row_send_to(way, step, chunk, src):
        offset = (1 - step) if way == 0 else (step - 1)
        send(
            src, strip(offset, core, chunk),
            row_recv.at[step - 1],
            row_next if way == 0 else row_prev,
        )

    def share_strip(offset, chunk, src):
        send(src, strip(offset, core, chunk), sib_recv, sibling)

    def row_own(chunk):
        src = row_block.at[:, pl.ds(chunk * wide, wide)]
        for way in range(2):
            if reach(chips, chunk)[way] >= 1:
                row_send_to(way, 1, chunk, src)

    def row_event(step):
        due = strips_due(chips, step) * wide // cols
        arrived(strips.at[pl.ds(0, due * depth)], row_recv.at[step - 1])
        for chunk in range(ROW_CHUNKS):
            for way, limit in enumerate(reach(chips, chunk)):
                if step <= limit:
                    offset = -step if way == 0 else step
                    slot = strip(offset, core, chunk)
                    if step < limit:
                        row_send_to(way, step + 1, chunk, slot)
                    share_strip(offset, chunk, slot)

    def make_upper(chunk):
        at = pl.ds(chunk * wide, wide)
        for i in range(order // BLOCK):
            end = (i + 1) * BLOCK
            upper[pl.ds(i * BLOCK, BLOCK), at] = jnp.dot(
                linv[pl.ds(i * BLOCK, BLOCK), pl.ds(0, end)],
                strips[pl.ds(0, end), at],
                preferred_element_type=jnp.float32,
            ).astype(jnp.bfloat16)

    def make_lower(chunk):
        at = pl.ds(*pieces[chunk])
        parts = [gathered[k, at] for k in range(n_col)]
        left = jnp.concatenate(parts, axis=1)
        for j in range(order // BLOCK):
            end = (j + 1) * BLOCK
            lower[at, pl.ds(j * BLOCK, BLOCK)] = jnp.dot(
                left[:, :end],
                uinv[pl.ds(0, end), pl.ds(j * BLOCK, BLOCK)],
                preferred_element_type=jnp.float32,
            ).astype(jnp.bfloat16)
        if share % 128 == 0:
            lower_tile[at] = lower[at, pl.ds(pl.multiple_of(col * share, share), share)]
        else:
            for k in range(n_col):
                @pl.when(col == k)
                def _():
                    lower_tile[at] = lower[at, pl.ds(k * share, share)]

    def subtract(chunk):
        at = pl.ds(*pieces[chunk])
        updated[at] -= jnp.dot(lower[at], upper[...], preferred_element_type=jnp.float32)

    pl.when(even & (prev_row < row))(lambda: reply(1, row_prev))
    pl.when(even & (next_row < row))(lambda: reply(1, row_next))
    pl.when(even & (core == 1))(lambda: reply(1, sibling))
    mine_c.wait()
    pl.when(has_after)(lambda: await_reply(0))
    col_own(0, has_after)
    late = (3 - core - below) * (1 - odd)
    pl.when(late > 0)(lambda: pl.semaphore_wait(met.at[1], late))

    @pl.when(even & has_after)
    def _():
        for device in (row_next, row_prev, sibling):
            reply(2, device)

    pl.when(odd == 1)(lambda: await_reply(1))
    turn_own()
    for chunk in range(ROW_CHUNKS):
        row_own(chunk)
    load_t.start()
    for chunk in range(ROW_CHUNKS):
        share_strip(0, chunk, row_block.at[:, pl.ds(chunk * wide, wide)])

    @pl.when(even & has_after)
    def _():
        pl.semaphore_wait(met.at[2], 3)
        reply(1, after)

    row_depth = max(max(reach(chips, r)) for r in range(ROW_CHUNKS))
    last = len(pieces) - 1
    col_left = [(step, k) for step in range(2, n_col - 1) for k in range(len(pieces))]
    for chunk in range(2):
        col_event(1, chunk, 0)
    col_wait(1, 1, 1)

    @pl.when(held)
    def _():
        load_l.start()
        load_l.wait()

    col_event(1, 0, 1)
    col_pass(1, 1, 1)
    for chunk in range(2, len(pieces)):
        col_event(1, chunk)
    row_event(1)
    for group in turn_groups(chips):
        turn_event(*group)
    for step in range(2, row_depth + 1):
        if col_left:
            col_event(*col_left.pop(0))
        row_event(step)
    if col_left:
        col_event(*col_left.pop(0))
    arrived(strips.at[pl.ds(0, chips * depth)], sib_recv)
    mine_r.wait()
    pl.when(free)(lambda: load_l.wait())
    load_u.wait()
    for chunk in range(ROW_CHUNKS):
        make_upper(chunk)
        if col_left:
            col_event(*col_left.pop(0))
    for step, chunk in col_left:
        col_event(step, chunk)
    load_t.wait()
    turn_last()
    for chunk in range(len(pieces)):
        if chunk == last:
            drain()
        col_event(n_col - 1, chunk)
        if chunk < last:
            make_lower(chunk)
            subtract(chunk)


def finish(
    n_col, lower_done, gathered, uinv, upper, partial, lower_tile, upper_tile, updated,
    low, tile, rest, sem,
):
    rows, cols = partial.shape
    share = lower_tile.shape[1]
    depth = upper_tile.shape[0]
    order = uinv.shape[0]
    col = lax.axis_index("col")
    start = pl.multiple_of(lax.axis_index("row") * depth, depth)
    begin, size = chunks_of(rows)[-1]
    at, done = pl.ds(begin, size), pl.ds(0, begin)

    def copy(index, src, dst):
        pltpu.make_async_copy(src, dst, sem.at[index]).start()

    copy(0, partial.at[done], updated.at[done])
    copy(1, lower_done.at[done], lower_tile.at[done])
    copy(2, upper.at[pl.ds(start, depth)], upper_tile)
    left = jnp.concatenate([gathered[k, at] for k in range(n_col)], axis=1)
    for j in range(order // BLOCK):
        end = (j + 1) * BLOCK
        low[:, pl.ds(j * BLOCK, BLOCK)] = jnp.dot(
            left[:, :end],
            uinv[pl.ds(0, end), pl.ds(j * BLOCK, BLOCK)],
            preferred_element_type=jnp.float32,
        ).astype(jnp.bfloat16)
    if share % 128 == 0:
        tile[...] = low[:, pl.ds(pl.multiple_of(col * share, share), share)]
    else:
        for k in range(n_col):
            @pl.when(col == k)
            def _():
                tile[...] = low[:, pl.ds(k * share, share)]
    copy(1, tile, lower_tile.at[at])
    for j in range(cols // BLOCK):
        across = pl.ds(j * BLOCK, BLOCK)
        rest[:, across] = partial[at, across] - jnp.dot(
            low[...], upper[:, across], preferred_element_type=jnp.float32
        )
        copy(0, rest.at[:, across], updated.at[at, across])
    for index, whole in enumerate((updated, lower_tile, upper_tile)):
        pltpu.make_async_copy(whole, whole, sem.at[index]).wait()


def on_device(n_row, n_col, trailing, column_block, row_block, lower_inv, upper_inv):
    rows, share = column_block.shape
    depth, cols = row_block.shape
    order = lower_inv.shape[0]
    chips = n_row // 2
    narrow = jnp.bfloat16
    hbm = pl.BlockSpec(memory_space=pltpu.HBM)
    inside = pl.BlockSpec(memory_space=pltpu.VMEM)
    dma = pltpu.SemaphoreType.DMA
    count = len(PARTS)
    last = chunks_of(rows)[-1][1]
    inputs = (trailing, column_block, row_block, lower_inv, upper_inv)
    tile = jax.ShapeDtypeStruct((rows, share), narrow)
    whole = jax.ShapeDtypeStruct((rows, cols), jnp.float32)
    lower_done, gathered, uinv, upper, partial = pl.pallas_call(
        functools.partial(kernel, n_row, n_col),
        out_shape=(
            tile,
            jax.ShapeDtypeStruct((n_col, rows, share), narrow),
            jax.ShapeDtypeStruct((order, order), narrow),
            jax.ShapeDtypeStruct((order, cols), narrow),
            whole,
        ),
        in_specs=[hbm] * 5,
        out_specs=(inside,) * 5,
        scratch_shapes=[
            pltpu.VMEM((order, cols), narrow),
            pltpu.VMEM((order, order), narrow),
            pltpu.VMEM((rows, order), narrow),
            pltpu.VMEM((len(turn_stops(chips)), rows // DETOUR, share), narrow),
            dma((5,)),
            dma((2,)),
            dma((n_col - 1, count)),
            dma,
            dma((chips // 2,)),
            dma,
            dma,
            dma,
            pltpu.SemaphoreType.REGULAR((3,)),
        ],
        compiler_params=pltpu.CompilerParams(
            collective_id=0, has_side_effects=True, vmem_limit_bytes=32 << 20
        ),
    )(*(pltpu.with_memory_space_constraint(x, pltpu.HBM) for x in inputs))
    return pl.pallas_call(
        functools.partial(finish, n_col),
        out_shape=(tile, jax.ShapeDtypeStruct((depth, cols), narrow), whole),
        in_specs=[inside] * 5,
        out_specs=(hbm,) * 3,
        scratch_shapes=[
            pltpu.VMEM((last, order), narrow),
            pltpu.VMEM((last, share), narrow),
            pltpu.VMEM((last, cols), jnp.float32),
            dma((3,)),
        ],
        compiler_params=pltpu.CompilerParams(vmem_limit_bytes=16 << 20),
    )(lower_done, gathered, uinv, upper, partial)


def solution(mesh):
    specs = P("row", "col")
    return jax.shard_map(
        functools.partial(on_device, mesh.shape["row"], mesh.shape["col"]),
        mesh=mesh,
        in_specs=(specs, specs, specs, P(), P()),
        out_specs=(specs,) * 3,
        check_vma=False,
    )
```

```python
import functools

import jax
import jax.numpy as jnp
from jax import lax
from jax.experimental import pallas as pl
from jax.experimental.pallas import tpu as pltpu
from jax.sharding import PartitionSpec as P

MESH = pl.DeviceIdType.MESH
BLOCK = 256
PARTS = (5, 4, 3)
ROW_CHUNKS = 2
DETOUR = 24


def chunks_of(rows):
    unit = rows // sum(PARTS)
    starts = [sum(PARTS[:k]) * unit for k in range(len(PARTS))]
    return [(start, part * unit) for start, part in zip(starts, PARTS)]


def reach(size, chunk):
    each = (size - 1) // 2
    extra = 1 if size % 2 == 0 else 0
    return (each + extra, each) if chunk % 2 == 0 else (each, each + extra)


def strips_due(chips, step):
    return sum(limit >= step for r in range(ROW_CHUNKS) for limit in reach(chips, r))


def turn_stops(chips):
    return [(1,), (1, 2), (chips - 1,)] if chips > 3 else [(1,), (chips - 1,)]


def turn_groups(chips):
    groups = {}
    for side, stops in enumerate(turn_stops(chips)):
        for hop, stop in enumerate(stops):
            groups.setdefault((hop, stop), []).append(side)
    return [(hop, stop, sides) for (hop, stop), sides in sorted(groups.items())]


def kernel(
    n_row, n_col,
    trailing, column_block, row_block, lower_inv, upper_inv,
    lower_tile, gathered, uinv, upper, updated,
    strips, linv, lower, spare,
    local_sem, col_send, col_recv, row_send, row_recv, sib_recv, spare_send, spare_recv, met,
):
    rows, share = column_block.shape
    depth, cols = row_block.shape
    order = lower_inv.shape[0]
    pieces = chunks_of(rows)
    wide = cols // ROW_CHUNKS
    row, col = lax.axis_index("row"), lax.axis_index("col")
    chips = n_row // 2
    core = lax.rem(row, 2)
    after = {"col": col + 1}
    before = {"col": col - 1}
    has_after = col < n_col - 1
    has_before = col > 0

    barrier = pltpu.get_barrier_semaphore()

    def greet(device):
        pl.semaphore_signal(barrier, inc=1, device_id=device, device_id_type=MESH)

    odd = lax.rem(col, 2)
    even = odd == 0
    held = even & (core == 1)
    free = (odd == 1) | (core == 0)

    def reply(index, device):
        pl.semaphore_signal(met.at[index], inc=1, device_id=device, device_id_type=MESH)

    def await_reply(index):
        pl.semaphore_wait(met.at[index], 1)

    pl.when(has_after)(lambda: greet(after))

    @pl.when(odd == 1)
    def _():
        pl.semaphore_wait(barrier, 1)
        reply(0, before)


    def arrived(dst, sem):
        pltpu.make_async_copy(dst, dst, sem).wait()

    turn = rows // DETOUR
    stops = turn_stops(chips)

    def span(chunk, short):
        start, size = pieces[chunk]
        return pl.ds(start, size - len(stops) * turn if short else size)

    def col_slot(owner, chunk, short=False):
        return gathered.at[owner, span(chunk, short)]

    def col_copy(way, step, chunk, short=False):
        owner = col + (1 - step if way == 0 else step - 1)
        slot = col_slot(owner, chunk, short)
        straight = step == 1 and way == 1
        return pltpu.make_async_remote_copy(
            src_ref=column_block.at[span(chunk, short)] if straight else slot,
            dst_ref=slot,
            send_sem=col_send.at[way],
            recv_sem=col_recv.at[owner - way, chunk],
            device_id=after if way == 0 else before,
            device_id_type=MESH,
        )

    def sends(way, step):
        if way == 0:
            return has_after if step == 1 else has_after & (col >= step - 1)
        return has_before if step == 1 else has_before & (col + step - 1 < n_col)

    def takes(way, step):
        return col >= step if way == 0 else col + step < n_col

    def col_own(way, where, bends=0):
        for short in reversed(range(1 + bends)):
            @pl.when(sends(way, 1) & where & turns(1, short) if bends else sends(way, 1) & where)
            def _():
                for chunk in range(len(pieces)):
                    col_copy(way, 1, chunk, short and chunk == 0).start()

    def turns(at, short):
        return (row < 2) & (col == at) if short else (row >= 2) | (col != at)

    col_own(1, odd == 1, 1)
    half = chips // 2

    def snake(place):
        return place + (place // half) * (chips + half - 1 - 2 * place)

    place = snake(row // 2)

    def chip_at(offset):
        return snake(lax.rem(place + chips + offset, chips))

    sibling = {"row": row + 1 - 2 * core}
    next_row = chip_at(1) * 2 + core
    prev_row = chip_at(-1) * 2 + core
    row_next = {"row": next_row}
    row_prev = {"row": prev_row}
    next_later = next_row > row
    prev_later = prev_row > row
    load_l = pltpu.make_async_copy(lower_inv, linv, local_sem.at[0])
    load_u = pltpu.make_async_copy(upper_inv, uinv, local_sem.at[1])
    load_t = pltpu.make_async_copy(trailing, updated, local_sem.at[2])
    mine_c = pltpu.make_async_copy(column_block, gathered.at[col], local_sem.at[3])
    my_rows = pl.ds(pl.multiple_of(row * depth, depth), depth)
    mine_r = pltpu.make_async_copy(row_block, strips.at[my_rows], local_sem.at[4])

    pl.when(even & next_later)(lambda: greet(row_next))
    pl.when(even & prev_later)(lambda: greet(row_prev))
    pl.when(even & (core == 0))(lambda: greet(sibling))
    mine_c.start()
    mine_r.start()
    below = (row - next_row + n_row) // n_row + (row - prev_row + n_row) // n_row
    early = ((col + n_col - 1) // n_col + core + below) * (1 - odd)
    pl.when(early > 0)(lambda: pl.semaphore_wait(barrier, early))
    pl.when(even & has_before)(lambda: reply(0, before))
    col_own(1, even)

    def send(src, dst, recv_sem, device):
        pltpu.make_async_remote_copy(
            src_ref=src, dst_ref=dst, send_sem=row_send, recv_sem=recv_sem,
            device_id=device, device_id_type=MESH,
        ).start()

    def turned(side):
        return pl.ds(pieces[0][1] - (len(stops) - side) * turn, turn)

    def turn_copy(src, dst, send_sem, device):
        pltpu.make_async_remote_copy(
            src_ref=src, dst_ref=dst, send_sem=send_sem, recv_sem=spare_recv,
            device_id=device, device_id_type=MESH,
        ).start()

    def turn_own():
        @pl.when(turns(1, True))
        def _():
            for side in range(len(stops)):
                turn_copy(
                    column_block.at[turned(side)], spare.at[side], col_send.at[1],
                    row_next if stops[side][0] == 1 else row_prev,
                )

    def turning(stop):
        return (place == stop) & (col == 1)

    def turn_block(sides):
        return spare.at[pl.ds(sides[0], len(sides))]

    def turn_event(hop, stop, sides):
        @pl.when(turning(stop))
        def _():
            arrived(turn_block(sides), spare_recv)
            for side in sides:
                if hop + 1 < len(stops[side]):
                    turn_copy(spare.at[side], spare.at[side], spare_send, row_next)
                else:
                    turn_copy(
                        spare.at[side], gathered.at[1, turned(side)], spare_send,
                        {"row": chip_at(-stop) * 2 + core, "col": col - 1},
                    )

    def turn_last():
        @pl.when(turns(0, True))
        def _():
            size = len(stops) * turn
            arrived(gathered.at[1, pl.ds(pieces[0][1] - size, size)], spare_recv)

    def lanes(lane):
        return (core >= 0) if lane is None else (core == lane)

    def col_wait(step, chunk, lane=None):
        mine = lanes(lane)
        for way in range(2):
            cut = way == 1 and step == 1 and chunk == 0
            for short in range(1 + cut):
                @pl.when(mine & (takes(way, step) & turns(0, short) if cut else takes(way, step)))
                def _():
                    owner = col - step if way == 0 else col + step
                    arrived(col_slot(owner, chunk, short), col_recv.at[owner - way, chunk])

    def col_pass(step, chunk, lane=None):
        if step < n_col - 1:
            for way in range(2):
                @pl.when(lanes(lane) & sends(way, step + 1))
                def _():
                    col_copy(way, step + 1, chunk).start()

    def col_event(step, chunk, lane=None):
        col_wait(step, chunk, lane)
        col_pass(step, chunk, lane)

    def drain():
        for count in range(1, n_col):
            block = gathered.at[pl.ds(0, count)]
            pl.when(col + 1 == count)(lambda: arrived(block, col_send.at[0]))
            pl.when(n_col - col == count)(lambda: arrived(block, col_send.at[1]))
        arrived(strips.at[pl.ds(0, (n_row - 1) * depth)], row_send)
        for hop, stop, sides in turn_groups(chips):
            pl.when(turning(stop))(lambda: arrived(turn_block(sides), spare_send))

    def strip(offset, lane, chunk):
        owner = chip_at(offset) * 2 + lane
        start = pl.multiple_of(owner * depth, depth)
        return strips.at[pl.ds(start, depth), pl.ds(chunk * wide, wide)]

    def row_send_to(way, step, chunk, src):
        offset = (1 - step) if way == 0 else (step - 1)
        send(
            src, strip(offset, core, chunk),
            row_recv.at[step - 1],
            row_next if way == 0 else row_prev,
        )

    def share_strip(offset, chunk, src):
        send(src, strip(offset, core, chunk), sib_recv, sibling)

    def row_own(chunk):
        src = row_block.at[:, pl.ds(chunk * wide, wide)]
        for way in range(2):
            if reach(chips, chunk)[way] >= 1:
                row_send_to(way, 1, chunk, src)

    def row_event(step):
        due = strips_due(chips, step) * wide // cols
        arrived(strips.at[pl.ds(0, due * depth)], row_recv.at[step - 1])
        for chunk in range(ROW_CHUNKS):
            for way, limit in enumerate(reach(chips, chunk)):
                if step <= limit:
                    offset = -step if way == 0 else step
                    slot = strip(offset, core, chunk)
                    if step < limit:
                        row_send_to(way, step + 1, chunk, slot)
                    share_strip(offset, chunk, slot)

    def make_upper(chunk):
        at = pl.ds(chunk * wide, wide)
        for i in range(order // BLOCK):
            end = (i + 1) * BLOCK
            upper[pl.ds(i * BLOCK, BLOCK), at] = jnp.dot(
                linv[pl.ds(i * BLOCK, BLOCK), pl.ds(0, end)],
                strips[pl.ds(0, end), at],
                preferred_element_type=jnp.float32,
            ).astype(jnp.bfloat16)

    def make_lower(chunk):
        at = pl.ds(*pieces[chunk])
        parts = [gathered[k, at] for k in range(n_col)]
        left = jnp.concatenate(parts, axis=1)
        for j in range(order // BLOCK):
            end = (j + 1) * BLOCK
            lower[at, pl.ds(j * BLOCK, BLOCK)] = jnp.dot(
                left[:, :end],
                uinv[pl.ds(0, end), pl.ds(j * BLOCK, BLOCK)],
                preferred_element_type=jnp.float32,
            ).astype(jnp.bfloat16)
        if share % 128 == 0:
            lower_tile[at] = lower[at, pl.ds(pl.multiple_of(col * share, share), share)]
        else:
            for k in range(n_col):
                @pl.when(col == k)
                def _():
                    lower_tile[at] = lower[at, pl.ds(k * share, share)]

    def subtract(chunk):
        at = pl.ds(*pieces[chunk])
        updated[at] -= jnp.dot(lower[at], upper[...], preferred_element_type=jnp.float32)

    pl.when(even & (prev_row < row))(lambda: reply(1, row_prev))
    pl.when(even & (next_row < row))(lambda: reply(1, row_next))
    pl.when(even & (core == 1))(lambda: reply(1, sibling))
    mine_c.wait()
    pl.when(has_after)(lambda: await_reply(0))
    col_own(0, has_after)
    late = (3 - core - below) * (1 - odd)
    pl.when(late > 0)(lambda: pl.semaphore_wait(met.at[1], late))

    @pl.when(even & has_after)
    def _():
        for device in (row_next, row_prev, sibling):
            reply(2, device)

    pl.when(odd == 1)(lambda: await_reply(1))
    turn_own()
    for chunk in range(ROW_CHUNKS):
        row_own(chunk)
    pl.when(free)(lambda: load_l.start())
    load_u.start()
    load_t.start()
    for chunk in range(ROW_CHUNKS):
        share_strip(0, chunk, row_block.at[:, pl.ds(chunk * wide, wide)])

    @pl.when(even & has_after)
    def _():
        pl.semaphore_wait(met.at[2], 3)
        reply(1, after)

    row_depth = max(max(reach(chips, r)) for r in range(ROW_CHUNKS))
    last = len(pieces) - 1
    col_left = [(step, k) for step in range(2, n_col - 1) for k in range(len(pieces))]
    for chunk in range(2):
        col_event(1, chunk, 0)
    col_wait(1, 1, 1)

    @pl.when(held)
    def _():
        load_l.start()
        load_l.wait()

    col_event(1, 0, 1)
    col_pass(1, 1, 1)
    for chunk in range(2, len(pieces)):
        col_event(1, chunk)
    row_event(1)
    for group in turn_groups(chips):
        turn_event(*group)
    for step in range(2, row_depth + 1):
        if col_left:
            col_event(*col_left.pop(0))
        row_event(step)
    if col_left:
        col_event(*col_left.pop(0))
    arrived(strips.at[pl.ds(0, chips * depth)], sib_recv)
    mine_r.wait()
    pl.when(free)(lambda: load_l.wait())
    load_u.wait()
    for chunk in range(ROW_CHUNKS):
        make_upper(chunk)
        if col_left:
            col_event(*col_left.pop(0))
    for step, chunk in col_left:
        col_event(step, chunk)
    load_t.wait()
    turn_last()
    for chunk in range(len(pieces)):
        if chunk == last:
            drain()
        col_event(n_col - 1, chunk)
        if chunk < last:
            make_lower(chunk)
            subtract(chunk)


def finish(
    n_col, lower_done, gathered, uinv, upper, partial, lower_tile, upper_tile, updated,
    low, tile, rest, sem,
):
    rows, cols = partial.shape
    share = lower_tile.shape[1]
    depth = upper_tile.shape[0]
    order = uinv.shape[0]
    col = lax.axis_index("col")
    start = pl.multiple_of(lax.axis_index("row") * depth, depth)
    begin, size = chunks_of(rows)[-1]
    at, done = pl.ds(begin, size), pl.ds(0, begin)

    def copy(index, src, dst):
        pltpu.make_async_copy(src, dst, sem.at[index]).start()

    copy(0, partial.at[done], updated.at[done])
    copy(1, lower_done.at[done], lower_tile.at[done])
    copy(2, upper.at[pl.ds(start, depth)], upper_tile)
    left = jnp.concatenate([gathered[k, at] for k in range(n_col)], axis=1)
    for j in range(order // BLOCK):
        end = (j + 1) * BLOCK
        low[:, pl.ds(j * BLOCK, BLOCK)] = jnp.dot(
            left[:, :end],
            uinv[pl.ds(0, end), pl.ds(j * BLOCK, BLOCK)],
            preferred_element_type=jnp.float32,
        ).astype(jnp.bfloat16)
    if share % 128 == 0:
        tile[...] = low[:, pl.ds(pl.multiple_of(col * share, share), share)]
    else:
        for k in range(n_col):
            @pl.when(col == k)
            def _():
                tile[...] = low[:, pl.ds(k * share, share)]
    copy(1, tile, lower_tile.at[at])
    for j in range(cols // BLOCK):
        across = pl.ds(j * BLOCK, BLOCK)
        rest[:, across] = partial[at, across] - jnp.dot(
            low[...], upper[:, across], preferred_element_type=jnp.float32
        )
        copy(0, rest.at[:, across], updated.at[at, across])
    for index, whole in enumerate((updated, lower_tile, upper_tile)):
        pltpu.make_async_copy(whole, whole, sem.at[index]).wait()


def on_device(n_row, n_col, trailing, column_block, row_block, lower_inv, upper_inv):
    rows, share = column_block.shape
    depth, cols = row_block.shape
    order = lower_inv.shape[0]
    chips = n_row // 2
    narrow = jnp.bfloat16
    hbm = pl.BlockSpec(memory_space=pltpu.HBM)
    inside = pl.BlockSpec(memory_space=pltpu.VMEM)
    dma = pltpu.SemaphoreType.DMA
    count = len(PARTS)
    last = chunks_of(rows)[-1][1]
    inputs = (trailing, column_block, row_block, lower_inv, upper_inv)
    tile = jax.ShapeDtypeStruct((rows, share), narrow)
    whole = jax.ShapeDtypeStruct((rows, cols), jnp.float32)
    lower_done, gathered, uinv, upper, partial = pl.pallas_call(
        functools.partial(kernel, n_row, n_col),
        out_shape=(
            tile,
            jax.ShapeDtypeStruct((n_col, rows, share), narrow),
            jax.ShapeDtypeStruct((order, order), narrow),
            jax.ShapeDtypeStruct((order, cols), narrow),
            whole,
        ),
        in_specs=[hbm] * 5,
        out_specs=(inside,) * 5,
        scratch_shapes=[
            pltpu.VMEM((order, cols), narrow),
            pltpu.VMEM((order, order), narrow),
            pltpu.VMEM((rows, order), narrow),
            pltpu.VMEM((len(turn_stops(chips)), rows // DETOUR, share), narrow),
            dma((5,)),
            dma((2,)),
            dma((n_col - 1, count)),
            dma,
            dma((chips // 2,)),
            dma,
            dma,
            dma,
            pltpu.SemaphoreType.REGULAR((3,)),
        ],
        compiler_params=pltpu.CompilerParams(
            collective_id=0, has_side_effects=True, vmem_limit_bytes=32 << 20
        ),
    )(*(pltpu.with_memory_space_constraint(x, pltpu.HBM) for x in inputs))
    return pl.pallas_call(
        functools.partial(finish, n_col),
        out_shape=(tile, jax.ShapeDtypeStruct((depth, cols), narrow), whole),
        in_specs=[inside] * 5,
        out_specs=(hbm,) * 3,
        scratch_shapes=[
            pltpu.VMEM((last, order), narrow),
            pltpu.VMEM((last, share), narrow),
            pltpu.VMEM((last, cols), jnp.float32),
            dma((3,)),
        ],
        compiler_params=pltpu.CompilerParams(vmem_limit_bytes=16 << 20),
    )(lower_done, gathered, uinv, upper, partial)


def solution(mesh):
    specs = P("row", "col")
    return jax.shard_map(
        functools.partial(on_device, mesh.shape["row"], mesh.shape["col"]),
        mesh=mesh,
        in_specs=(specs, specs, specs, P(), P()),
        out_specs=(specs,) * 3,
        check_vma=False,
    )
```
